32 devices in a mesh: parts: 2 (over y), branch: 4 (over z), heads: 4 (over x, core).
Axes of the slice: x: 2, y: 2, z: 4, core: 2. Of those that a mesh axis runs over, the one named last changes fastest.
Arguments:
- residual: bfloat16 [64, 5120], P('parts', ('branch', 'heads')), parts along dimension 0, may hold values from -6 to 6
- arrival: int32 [64], P('parts'), parts along dimension 0, may hold values from 0 to 31, each once
- lengths: int32 [64], P('parts'), parts along dimension 0, may hold values from 2 to 2048
- norm_gain: bfloat16 [5120], P(('branch', 'heads')), may hold values from 0.5 to 1.5
- w_query: bfloat16 [5120, 4096], P('branch', 'heads')
- w_keyval: bfloat16 [5120, 2048], P('branch', 'heads'), may hold values from -0.078125 to 0.078125
- w_ssm_x: bfloat16 [5120, 4096], P('branch', 'heads'), may hold values from -0.078125 to 0.078125
- w_ssm_z: bfloat16 [5120, 4096], P('branch', 'heads'), may hold values from -0.078125 to 0.078125
- w_write_read: bfloat16 [5120, 512], P('branch'), may hold values from -0.078125 to 0.078125
- w_dt: bfloat16 [5120, 64], P('branch', 'heads'), may hold values from -0.078125 to 0.078125
- dt_bias: float32 [64], P('heads'), may hold values from -3 to 0
- a_rate: float32 [64], P('heads'), may hold values from 0.3 to 8
- skip_gain: float32 [64], P('heads'), may hold values from 0.5 to 1.5
- ssm_gain: float32 [4096], P('heads'), may hold values from 0.5 to 1.5
- w_out_att: bfloat16 [4096, 5120], P('heads', 'branch'), may hold values from -0.09375 to 0.09375
- w_out_ssm: bfloat16 [4096, 5120], P('heads', 'branch'), may hold values from -0.09375 to 0.09375
- kv_cache: bfloat16 [64, 2048, 2048], P(('parts', 'branch'), 'heads'), parts along dimension 0, may hold values from -6 to 6
- ssm_state: float32 [64, 64, 64, 256], P(('parts', 'branch'), 'heads'), parts along dimension 0, may hold values from -6 to 6
Outputs:
- residual_out: bfloat16 [64, 5120], P('parts', ('branch', 'heads')), parts along dimension 0
- new_state: float32 [64, 64, 64, 256], P(('parts', 'branch'), 'heads'), parts along dimension 0
The draws below stay inside these ranges and needn't reach their ends.
There are 2 independent parts, one for each index of `parts`. The reference program is written for one: setup_inputs(seed, part) draws one part's arguments, and reference() takes and returns one part's arrays. A program takes and returns all parts, laid end to end along the dimension named above; an argument that names none is the same for every part. Nothing has to cross between parts.
All inputs are finite; a program needn't handle non-finite values.
Results may differ from the reference program's by a relative error of at most 0.0064.
Values may be sent and summed in bfloat16 or wider, within the bound.
A program may use at most 128 MiB of HBM per device.

```python
import math
import jax
import jax.numpy as jnp
from jax import lax

D = 5120
QH = 32
KVH = 8
HD = 128
SH = 64
SP = 64
NS = 256
L = 2048
REQ = 32
N_HEADS = 4


def draw_residual(key, part):
    values = jax.random.normal(jax.random.fold_in(key, 11), (REQ, D), jnp.float32)
    return jnp.clip(values, -6.0, 6.0).astype(jnp.bfloat16)


def draw_w_query(key, part):
    values = jnp.clip(jax.random.normal(jax.random.fold_in(key, 23), (D, QH * HD), jnp.float32), -6.0, 6.0) / math.sqrt(D)
    return values.astype(jnp.bfloat16)


def draw_kv_cache(key, part):
    base_key = jax.random.fold_in(key, 37)
    noise_key = jax.random.fold_in(base_key, 0)
    direction = jax.random.normal(jax.random.fold_in(base_key, 5), (REQ, 1, KVH * HD), jnp.float32)
    direction = jnp.clip(direction, -2.0, 2.0)
    ramp = jnp.arange(L).astype(jnp.float32) / L
    values = jax.random.normal(noise_key, (REQ, L, 2 * KVH * HD), jnp.float32)
    weight_pos = 0.3 + 1.5 * ramp
    shifted = values[:, :, KVH * HD:] + weight_pos[None, :, None] * direction
    values = values.at[:, :, KVH * HD:].set(shifted)
    return jnp.clip(values, -6.0, 6.0).astype(jnp.bfloat16)


def with_ends(values, stream_key, smallest, high):
    index_at = [jax.random.randint(jax.random.fold_in(stream_key, axis), (), 0, length) for axis, length in enumerate(values.shape)]
    main_axis = values.shape.index(max(values.shape))
    neighbour = index_at[:main_axis] + [(index_at[main_axis] + 1) % values.shape[main_axis]] + index_at[main_axis + 1:]
    return values.at[tuple(index_at)].set(smallest).at[tuple(neighbour)].set(high)


def steps_of(key, dims, cuts, least, largest):
    def one(axis_at, shards_of):
        heights = jax.random.uniform(jax.random.fold_in(jax.random.fold_in(key, 6), axis_at), (shards_of,), jnp.float32, least / len(cuts), largest / len(cuts))
        return jnp.repeat(jnp.exp(heights), dims[axis_at] // shards_of).reshape((-1,) + (1,) * (len(dims) - axis_at - 1))

    level = one(*cuts[0])
    for cut in cuts[1:]:
        level = level * one(*cut)
    return level


def normal_values(key, extent, spread, limit, pieces=(), kind=jnp.bfloat16):
    values = spread * jax.random.normal(key, extent, jnp.float32)
    if pieces:
        values = values * steps_of(key, extent, pieces, -0.22, 0.18)
    return jnp.clip(values, -limit, limit).astype(kind)


def setup_inputs(seed: int = 0, part: int = 0) -> dict:
    splits = jax.random.split(jax.random.key(seed), 19)
    part_keys = jax.random.split(jax.random.fold_in(splits[18], part), 19)
    return {
        "residual": draw_residual(jax.random.fold_in(jax.random.fold_in(splits[18], part), 71), part),
        "arrival": jax.random.permutation(part_keys[1], REQ).astype(jnp.int32),
        "lengths": with_ends(jax.random.randint(part_keys[2], (REQ,), 2, L + 1), jax.random.fold_in(part_keys[2], 1), 2, L).astype(jnp.int32),
        "norm_gain": jnp.clip(1.0 + 0.1 * jax.random.normal(splits[3], (D,), jnp.float32), 0.5, 1.5).astype(jnp.bfloat16),
        "w_query": draw_w_query(jax.random.fold_in(splits[18], 71), part),
        "w_keyval": normal_values(splits[5], (D, 2 * KVH * HD), D ** -0.5, 0.078125, ((0, 4), (1, 4))),
        "w_ssm_x": normal_values(splits[6], (D, SH * SP), D ** -0.5, 0.078125, ((0, 4), (1, 4))),
        "w_ssm_z": normal_values(splits[7], (D, SH * SP), D ** -0.5, 0.078125, ((0, 4), (1, 4))),
        "w_write_read": normal_values(splits[8], (D, 2 * NS), D ** -0.5, 0.078125, ((0, 4),)),
        "w_dt": normal_values(splits[9], (D, SH), D ** -0.5, 0.078125, ((0, 4), (1, 4))),
        "dt_bias": jnp.clip(-3.0 + 3.0 * jax.random.uniform(splits[10], (SH,), jnp.float32) ** steps_of(splits[10], (SH,), ((0, 4),), -0.2, 0.2), -3.0, 0.0),
        "a_rate": jnp.clip(jnp.exp(math.log(8.0) - 3.2834143 * jax.random.uniform(splits[11], (SH,), jnp.float32) ** steps_of(splits[11], (SH,), ((0, 4),), -0.2, 0.2)), 0.3, 8.0),
        "skip_gain": jnp.clip(0.5 + 1.0 * jax.random.uniform(splits[12], (SH,), jnp.float32) ** steps_of(splits[12], (SH,), ((0, 4),), -0.2, 0.2), 0.5, 1.5),
        "ssm_gain": jnp.clip(1.0 + 0.1 * jax.random.normal(splits[13], (SH * SP,), jnp.float32), 0.5, 1.5),
        "w_out_att": normal_values(splits[14], (QH * HD, D), (QH * HD) ** -0.5, 0.09375, ((0, 4), (1, 4))),
        "w_out_ssm": normal_values(splits[15], (SH * SP, D), (SH * SP) ** -0.5, 0.09375, ((0, 4), (1, 4))),
        "kv_cache": draw_kv_cache(jax.random.fold_in(jax.random.fold_in(splits[18], part), 71), part),
        "ssm_state": normal_values(part_keys[17], (REQ, SH, SP, NS), 1.0, 6.0, ((0, 4), (1, 4)), jnp.float32),
    }


def rounded(value):
    return lax.optimization_barrier(value.astype(jnp.bfloat16)).astype(jnp.float32)

def attend_one(item):
    queries, cache, length, new_keys, new_vals = item
    group = QH // KVH
    span_len = L // N_HEADS
    scaling = HD ** (-0.5)
    query_wide = queries.astype(jnp.float32).reshape(KVH, group, HD)
    keys_all = cache[:, :KVH * HD].astype(jnp.float32).reshape(N_HEADS, span_len, KVH, HD)
    vals_all = cache[:, KVH * HD:].astype(jnp.float32).reshape(N_HEADS, span_len, KVH, HD)
    scores = jnp.einsum('kgd,bskd->kgbs', query_wide, keys_all) * scaling
    position = jnp.arange(L).reshape(N_HEADS, span_len)
    valid = position < length
    scores = jnp.where(valid, scores, -1e+30)
    new_score = jnp.einsum('kgd,kd->kg', query_wide, new_keys.astype(jnp.float32).reshape(KVH, HD)) * scaling
    is_first = jnp.arange(N_HEADS) == 0
    block_max = jnp.maximum(lax.optimization_barrier(jnp.max(scores, axis=3)), jnp.where(is_first, new_score[..., None], -1e+30))
    weights = rounded(jnp.where(valid, jnp.exp(scores - block_max[..., None]), 0.0))
    new_weight = rounded(jnp.exp(new_score - block_max[..., 0]))
    overall = lax.optimization_barrier(jnp.max(block_max, axis=2))
    factor = jnp.exp(block_max - overall[..., None])
    totals = lax.optimization_barrier(jnp.sum(lax.optimization_barrier(jnp.sum(weights, axis=3)) * factor, axis=2)) + new_weight * factor[..., 0]
    summed = jnp.einsum('kgbs,bskd->kgbd', weights, vals_all)
    summed = lax.optimization_barrier(jnp.sum(summed * factor[..., None], axis=2))
    summed = summed + (new_weight * factor[..., 0])[..., None] * new_vals.astype(jnp.float32).reshape(KVH, 1, HD)
    return (summed / totals[..., None]).reshape(QH * HD)

def reference(residual, arrival, lengths, norm_gain, w_query, w_keyval, w_ssm_x, w_ssm_z, w_write_read, w_dt, dt_bias, a_rate, skip_gain, ssm_gain, w_out_att, w_out_ssm, kv_cache, ssm_state):
    count_rows = residual.shape[0]
    ordered = jnp.zeros_like(residual).at[arrival].set(residual)
    widened = ordered.astype(jnp.float32)
    mean_sq = lax.optimization_barrier(jnp.mean(widened * widened, axis=1, keepdims=True))
    normed = (widened * lax.rsqrt(mean_sq + 1e-05) * norm_gain.astype(jnp.float32)[None, :]).astype(jnp.bfloat16)
    query = jnp.dot(normed, w_query, preferred_element_type=jnp.float32).astype(jnp.bfloat16)
    new_kv = jnp.dot(normed, w_keyval, preferred_element_type=jnp.float32).astype(jnp.bfloat16)
    ssm_x = jnp.dot(normed, w_ssm_x, preferred_element_type=jnp.float32).astype(jnp.bfloat16)
    ssm_z = jnp.dot(normed, w_ssm_z, preferred_element_type=jnp.float32).astype(jnp.bfloat16)
    write_read = jnp.dot(normed, w_write_read, preferred_element_type=jnp.float32).astype(jnp.bfloat16)
    dt_raw = jnp.dot(normed, w_dt, preferred_element_type=jnp.float32)
    att = lax.map(attend_one, (query, kv_cache, lengths, new_kv[:, :KVH * HD], new_kv[:, KVH * HD:]))
    att_out = att.astype(jnp.bfloat16)
    step_size = jax.nn.softplus(dt_raw + dt_bias[None, :])
    decay = jnp.exp(-step_size * a_rate[None, :])
    inputs = ssm_x.astype(jnp.float32).reshape(count_rows, SH, SP)
    writes = write_read[:, :NS].astype(jnp.float32)
    reads = write_read[:, NS:].astype(jnp.float32)
    new_state = decay[:, :, None, None] * ssm_state + (step_size[:, :, None] * inputs)[..., None] * writes[:, None, None, :]
    output = jnp.einsum('rhpn,rn->rhp', new_state, reads, precision=lax.Precision.HIGHEST) + skip_gain[None, :, None] * inputs
    gated = output.reshape(count_rows, SH * SP) * jax.nn.silu(ssm_z.astype(jnp.float32))
    gate_ms = lax.optimization_barrier(jnp.mean(gated * gated, axis=1, keepdims=True))
    ssm_out = (gated * lax.rsqrt(gate_ms + 1e-05) * ssm_gain[None, :]).astype(jnp.bfloat16)
    update = jnp.dot(att_out, w_out_att, preferred_element_type=jnp.float32) + jnp.dot(ssm_out, w_out_ssm, preferred_element_type=jnp.float32)
    result = (widened + update).astype(jnp.bfloat16)
    return (result[arrival], new_state)
```

```python
import functools

import jax
import jax.numpy as jnp
from jax import lax
from jax.experimental import pallas as pl
from jax.experimental.pallas import tpu as pltpu
from jax.sharding import PartitionSpec as P

HD = 128
NEG = -1e30
SUM_LANE = 64
PARTS = 2
F32 = jnp.float32
BF16 = jnp.bfloat16
MIB = 1024 * 1024
NT = (((1,), (1,)), ((), ()))
TN = (((0,), (0,)), ((), ()))
MESH = pl.DeviceIdType.MESH


def dot(a, b):
    return jnp.dot(a, b, preferred_element_type=F32)


def iota(shape, dim):
    return lax.broadcasted_iota(jnp.int32, shape, dim)


def split3(v):
    a = v.astype(BF16).astype(F32)
    c = (v - a).astype(BF16).astype(F32)
    return a, c, v - a - c


class Links:
    def __init__(self, B, H):
        self.n = {"heads": H, "branch": B}
        self.me = {"heads": lax.axis_index("heads"), "branch": lax.axis_index("branch")}
        self.pending = []

    def to(self, axis, d):
        n, me = self.n[axis], self.me[axis]
        if axis == "heads" and n % 2 == 0:
            return lax.rem(me // 2 + d // 2, n // 2) * 2 + lax.rem(me + d % 2, 2)
        return lax.rem(me + d, n)

    def order(self, axis):
        n = self.n[axis]
        if axis == "heads":
            return list(range(n - 1, 0, -1))
        return sorted(range(1, n), key=lambda d: (-min(d, n - d), d))

    def greet(self):
        barrier = pltpu.get_barrier_semaphore()
        for axis in ("branch", "heads"):
            for d in self.order(axis):
                pl.semaphore_signal(barrier, 1, device_id={axis: self.to(axis, d)}, device_id_type=MESH)

    def greeted(self):
        pl.semaphore_wait(pltpu.get_barrier_semaphore(), self.n["heads"] + self.n["branch"] - 2)

    def push(self, src, dst, sems, k, axis, d):
        c = pltpu.make_async_remote_copy(
            src_ref=src, dst_ref=dst, send_sem=sems.at[0, k, d], recv_sem=sems.at[1, k, d],
            device_id={axis: self.to(axis, d)}, device_id_type=MESH,
        )
        c.start()
        self.pending.append(c)
        return c

    def drain(self):
        for c in self.pending:
            c.wait_send()
        self.pending = []


def attender(H, MR, h, q2, kvn, len_v, kv_v, keep):
    heads_all = q2.shape[0] // MR
    kw = kvn.shape[1] // 2
    kvh = kw // HD
    span = kv_v.shape[1]
    block_mask = iota((heads_all, kw), 0) // (heads_all // kvh) == iota((heads_all, kw), 1) // HD
    lane = iota((heads_all, HD), 1)
    pos = (h * span + iota((heads_all, span), 1)).astype(F32)
    scaling = HD ** (-0.5)
    is_first = h == 0

    def attend(r, mz):
        q = q2[pl.ds(r, heads_all, stride=MR), :]
        qb = jnp.where(block_mask, jnp.concatenate([q] * kvh, axis=1), 0.0)
        scores = lax.dot_general(qb.astype(BF16), kv_v[r, :, 0:kw], NT, preferred_element_type=F32) * scaling
        valid = pos < jnp.concatenate([len_v[pl.ds(r, 1), :]] * (span // HD), axis=1)
        scores = jnp.where(valid, scores, NEG)
        s_new = jnp.sum(qb * kvn[pl.ds(r, 1), 0:kw], axis=1, keepdims=True) * scaling
        top = jnp.maximum(jnp.max(scores, axis=1, keepdims=True), jnp.where(is_first, s_new, NEG))
        probs = jnp.where(valid, jnp.exp(scores - top), 0.0).astype(BF16)
        p_new = jnp.where(is_first, jnp.exp(s_new - top), 0.0).astype(BF16).astype(F32)
        z = jnp.sum(probs.astype(F32), axis=1, keepdims=True) + p_new
        o = dot(probs, kv_v[r, :, kw:2 * kw])
        o = jnp.where(block_mask, o + p_new * kvn[pl.ds(r, 1), kw:2 * kw], 0.0)
        acc = o[:, 0:HD]
        for e in range(1, kvh):
            acc = acc + o[:, e * HD:(e + 1) * HD]
        gl = heads_all // H
        for i in range(H):
            keep[i, r] = acc[i * gl:(i + 1) * gl]
        return jnp.where(lane == r, top, jnp.where(lane == MR + r, z, mz))

    return attend


def mixer_kernel(
    cfg,
    res, arr_row, lens, gain, dt_bias, a_rate, skip, ssm_gain, w_dt,
    w_q, w_kv, w_x, w_z, w_wr, w_oa, w_os, kv, st,
    out_res, st_v,
    wq_v, wkv_v, wx_v, wz_v, wwr_v, wdt_v, woa_v, wos_v, kv_v,
    res_v, arr_v, gain_v, lens_v, bias_v, rate_v, skip_v, sg_v,
    xin, xg, sb, rb, own, sm, rsm, qg, kvg, q2, kvn, wrn, len_v, ord_v, cols_v, wm,
    accs, accr, mzs, mzr, gss, gsr, at2, ge, ga, gsc, fs, fr,
    ssem, wsem, kvsem, stsem, asem, bsem, csem, dsem, esem, fsem,
):
    B, H, MR, NS = cfg
    R = B * MR
    links = Links(B, H)
    b, h = links.me["branch"], links.me["heads"]
    piece = res.shape[1]
    model = piece * H * B
    cq, ckv, cx, cz, cw = (w_q.shape[1], w_kv.shape[1], w_x.shape[1], w_z.shape[1], wwr_v.shape[1])
    split_wr = cw != w_wr.shape[1]
    o_wr = cq
    o_kv = o_wr + cw
    o_x = o_kv + ckv
    o_z = o_x + cx
    total_cols = o_z + cz
    hl = w_dt.shape[0]
    sp = cx // hl
    heads_all = cq * H // HD
    gl = cq // HD

    links.greet()
    small = [
        pltpu.make_async_copy(src, dst, ssem.at[i])
        for i, (src, dst) in enumerate((
            (res, res_v), (arr_row, arr_v), (gain, gain_v), (lens, lens_v), (dt_bias, bias_v), (a_rate, rate_v),
            (skip, skip_v), (ssm_gain, sg_v), (w_dt, wdt_v),
        ))
    ]
    for c in small[:3]:
        c.start()
    wr_src = w_wr.at[:, pl.ds(pl.multiple_of(h * cw, cw), cw)] if split_wr else w_wr
    weights = [
        pltpu.make_async_copy(src, dst, wsem.at[i])
        for i, (src, dst) in enumerate(((w_q, wq_v), (wr_src, wwr_v), (w_kv, wkv_v), (w_x, wx_v), (w_z, wz_v), (w_os, wos_v), (w_oa, woa_v)))
    ]
    for c in weights[:2] + small[3:] + weights[2:5]:
        c.start()
    for c in small[:3]:
        c.wait()

    perm = (iota((R, R), 0) == arr_v[...]).astype(BF16)
    rows = dot(perm, res_v[...])
    ord_v[...] = rows
    wide = xin.shape[2]
    sums = split3(jnp.sum(rows * rows, axis=1, keepdims=True))
    tail = jnp.zeros((R, wide - piece), F32)
    for i, part in enumerate(sums):
        tail = jnp.where(iota(tail.shape, 1) == i, part, tail)
    xin[0, :, 0:piece] = (rows * gain_v[...].reshape(1, piece).astype(F32)).astype(BF16)
    xin[0, :, piece:wide] = tail.astype(BF16)

    links.greeted()
    got = [links.push(xin.at[0], xin.at[d], asem, 0, "heads", d) for d in links.order("heads")]
    state_in = [pltpu.make_async_copy(st.at[r], st_v.at[r], stsem.at[r]) for r in range(MR)]
    cache_in = [pltpu.make_async_copy(kv.at[r], kv_v.at[r], kvsem.at[r]) for r in range(MR)]
    for c in cache_in + state_in + weights[5:]:
        c.start()
    for c in small[3:]:
        c.wait()
    mine = (iota((MR, R), 1) == b * MR + iota((MR, R), 0)).astype(F32)
    len_v[...] = jnp.broadcast_to(jnp.sum(mine * lens_v[...].astype(F32), axis=1, keepdims=True), (MR, HD))
    for c in got:
        c.wait_recv()

    def slot(i):
        if H % 2 == 0:
            dx = lax.rem(h // 2 - i // 2 + H // 2, H // 2)
            dc = lax.rem(h - i % 2 + 2, 2)
            return dx * 2 + dc
        return lax.rem(h - i + H, H)

    sumsq = jnp.zeros((R, 1), F32)
    for i in range(H):
        part = xin[slot(i)]
        xg[:, i * piece:(i + 1) * piece] = part[:, 0:piece]
        t = part[:, piece:wide].astype(F32)
        sumsq = sumsq + jnp.sum(jnp.where(iota(t.shape, 1) < 3, t, 0.0), axis=1, keepdims=True)
    x = xg[...]

    def project(i, w_ref, lo, hi):
        weights[i].wait()
        val = dot(x, w_ref[...])
        own[:, lo:hi] = val
        for j in range(B):
            sb[j, :, lo:hi] = val[j * MR:(j + 1) * MR].astype(BF16)

    def scatter(k, lo, hi):
        return [
            links.push(sb.at[lax.rem(b + d, B), :, lo:hi], rb.at[d, :, lo:hi], bsem, k, "branch", d)
            for d in links.order("branch")
        ]

    project(0, wq_v, 0, cq)
    project(1, wwr_v, o_wr, o_kv)
    got_q = scatter(0, 0, o_kv)
    sm[...] = jnp.broadcast_to(sumsq, (R, HD))
    sm[:, 0:hl] = lax.dot_general(x, wdt_v[...], NT, preferred_element_type=F32)
    got_small = [
        links.push(sm.at[pl.ds(pl.multiple_of(lax.rem(b + d, B) * MR, MR), MR), :], rsm.at[d], bsem, 1, "branch", d)
        for d in links.order("branch")
    ]
    project(2, wkv_v, o_kv, o_x)
    got_kv = scatter(2, o_kv, o_x)
    project(3, wx_v, o_x, o_z)
    project(4, wz_v, o_z, total_cols)
    my_rows = pl.ds(pl.multiple_of(b * MR, MR), MR)
    for c in got_small:
        c.wait_recv()
    tot = sm[my_rows, :]
    for d in range(1, B):
        tot = tot + rsm[d]
    scale = lax.rsqrt(tot[:, SUM_LANE:SUM_LANE + 1] / model + 1e-05)

    def reduced(lo, hi):
        val = own[my_rows, lo:hi]
        for d in range(1, B):
            val = val + rb[d, :, lo:hi].astype(F32)
        return (val * scale).astype(BF16)

    for c in got_q:
        c.wait_recv()
    qw = qg.shape[2]
    qg[h] = reduced(0, qw)
    got_a = [links.push(qg.at[h], qg.at[h], csem, 0, "heads", d) for d in links.order("heads")]
    if not split_wr:
        wrn[...] = reduced(o_wr, o_kv).astype(F32)
    for c in got_kv:
        c.wait_recv()
    kvg[h] = reduced(o_kv, o_x)
    got_b = [links.push(kvg.at[h], kvg.at[h], csem, 1, "heads", d) for d in links.order("heads")]
    got_xz = scatter(3, o_x, o_z) + scatter(4, o_z, total_cols)
    pre = tot[:, 0:hl] * scale + bias_v[...]
    step = jnp.maximum(pre, 0.0) + jnp.log1p(jnp.exp(-jnp.abs(pre)))
    decay = jnp.exp(-step * rate_v[...])
    spread = (iota((hl, cx), 1) // sp == iota((hl, cx), 0)).astype(F32)

    def widen(v):
        return jnp.dot(v, spread, preferred_element_type=F32, precision=lax.Precision.HIGHEST)

    decay_w = widen(decay)
    step_w = widen(step)
    skip_w = widen(jnp.broadcast_to(skip_v[...], (MR, hl)))
    for c in got_a:
        c.wait_recv()
    if split_wr:
        for i in range(H):
            wrn[:, i * cw:(i + 1) * cw] = qg[i, :, cq:cq + cw].astype(F32)
    for g in range(heads_all):
        q2[g * MR:(g + 1) * MR, :] = qg[g // gl, :, (g % gl) * HD:(g % gl + 1) * HD].astype(F32)
    for c in got_b:
        c.wait_recv()
    for i in range(H):
        kvn[:, i * ckv:(i + 1) * ckv] = kvg[i].astype(F32)
    attend = attender(H, MR, h, q2, kvn, len_v, kv_v, accs)
    mz = jnp.zeros((heads_all, HD), F32)
    got = []
    for k in range(PARTS):
        lo, hi = k * MR // PARTS, (k + 1) * MR // PARTS
        for r in range(lo, hi):
            cache_in[r].wait()
        for r in range(lo, hi):
            mz = attend(r, mz)
        for d in links.order("heads"):
            got.append(links.push(accs.at[links.to("heads", d), lo:hi], accr.at[d, lo:hi], dsem, k, "heads", d))
    for i in range(H):
        mzs[i] = mz[i * gl:(i + 1) * gl]
    for d in links.order("heads"):
        got.append(links.push(mzs.at[links.to("heads", d)], mzr.at[d], dsem, PARTS, "heads", d))
    write = wrn[:, 0:NS]
    read = wrn[:, NS:2 * NS]
    read_b = read.astype(BF16)
    row = iota((MR, cx), 0)
    for c in state_in:
        c.wait()

    def readout(r, y):
        part = lax.dot_general(read_b, st_v[r].astype(BF16), NT, preferred_element_type=F32)
        return jnp.where(row == r, part, y)

    y = lax.fori_loop(0, MR, readout, jnp.zeros((MR, cx), F32), unroll=2)
    for c in got_xz:
        c.wait_recv()
    ssm_x = reduced(o_x, o_z).astype(F32)
    ssm_z = reduced(o_z, total_cols).astype(F32)
    dtx = step_w * ssm_x
    y = decay_w * y + dtx * jnp.sum(write * read, axis=1, keepdims=True) + skip_w * ssm_x
    gated = y * (ssm_z * jax.nn.sigmoid(ssm_z))
    own_gate = jnp.broadcast_to(jnp.sum(gated * gated, axis=1, keepdims=True), (MR, HD))
    gss[...] = own_gate
    got_gate = [links.push(gss, gsr.at[d], dsem, PARTS + 1, "heads", d) for d in links.order("heads")]
    ge[b] = (gated * sg_v[...]).astype(BF16)
    got_e = [links.push(ge.at[b], ge.at[b], esem, 0, "branch", d) for d in links.order("branch")]
    dtx_hi = dtx.astype(BF16).astype(F32)
    cols_v[...] = jnp.transpose(jnp.concatenate([dtx_hi, dtx - dtx_hi, decay_w], axis=0))
    turn = lax.rem(iota((2 * MR, NS), 0), MR)
    for r in range(MR):
        wm[:, r * NS:(r + 1) * NS] = jnp.where(turn == r, wrn[r:r + 1, 0:NS], 0.0).astype(BF16)
    for c in got:
        c.wait_recv()
    accr[0] = accs[h]
    mzr[0] = mzs[h]
    for r in range(MR):
        tops = [mzr[i][:, r:r + 1] for i in range(H)]
        best = functools.reduce(jnp.maximum, tops)
        num = jnp.zeros((gl, HD), F32)
        den = jnp.zeros((gl, 1), F32)
        for i in range(H):
            f = jnp.exp(tops[i] - best)
            num = num + f * accr[i, r]
            den = den + f * mzr[i][:, MR + r:MR + r + 1]
        at2[pl.ds(r, gl, stride=MR), :] = num / den
    for g in range(gl):
        ga[b, :, g * HD:(g + 1) * HD] = at2[g * MR:(g + 1) * MR, :].astype(BF16)
    got_a = [links.push(ga.at[b], ga.at[b], esem, 1, "branch", d) for d in links.order("branch")]
    for c in got_gate:
        c.wait_recv()
    gate = own_gate
    for d in range(1, H):
        gate = gate + gsr[d]
    gsc[b] = lax.rsqrt(gate / (cx * H) + 1e-05)
    got_a += [links.push(gsc.at[b], gsc.at[b], esem, 2, "branch", d) for d in links.order("branch")]

    def renew(i, carry):
        at = pl.multiple_of(i * sp, sp)
        lhs = cols_v[pl.ds(at, sp), 0:2 * MR].astype(BF16)
        keep = cols_v[pl.ds(at, 1), :]
        for r in range(MR):
            st_v[r, pl.ds(at, sp), :] = (
                keep[:, 2 * MR + r:2 * MR + r + 1] * st_v[r, pl.ds(at, sp), :] + dot(lhs, wm[:, r * NS:(r + 1) * NS])
            )
        return carry

    def stacked(ref):
        return jnp.concatenate([ref[i].astype(F32) for i in range(B)], axis=0)

    cut = hl - hl // 4
    lax.fori_loop(0, cut, renew, 0, unroll=4 if cut % 4 == 0 else 1)
    for c in weights[5:]:
        c.wait()
    for c in got_e:
        c.wait_recv()
    ssm_part = dot(stacked(ge).astype(BF16), wos_v[...])
    links.drain()
    for c in got_a:
        c.wait_recv()
    part = dot(stacked(ga).astype(BF16), woa_v[...]) + ssm_part * stacked(gsc)[:, 0:1]
    for i in range(H):
        fs[i] = part[:, i * piece:(i + 1) * piece].astype(fs.dtype)
    got = [links.push(fs.at[links.to("heads", d)], fr.at[d], fsem, 0, "heads", d) for d in links.order("heads")]
    lax.fori_loop(cut, hl, renew, 0, unroll=4 if (hl - cut) % 4 == 0 else 1)
    total = ord_v[...] + fs[h].astype(F32)
    for c in got:
        c.wait_recv()
    for d in range(1, H):
        total = total + fr[d].astype(F32)
    out_res[...] = lax.dot_general(perm, total.astype(BF16), TN, preferred_element_type=F32).astype(BF16)
    links.drain()


def deliver_kernel(res, st, out_res, out_st, sem):
    copies = [pltpu.make_async_copy(res, out_res, sem.at[0])]
    for r in range(st.shape[0]):
        copies.append(pltpu.make_async_copy(st.at[r], out_st.at[r], sem.at[r + 1]))
    for c in copies:
        c.start()
    for c in copies:
        c.wait()


def body(
    B, H,
    residual, arrival, lengths, norm_gain, w_query, w_keyval, w_ssm_x, w_ssm_z, w_write_read, w_dt,
    dt_bias, a_rate, skip_gain, ssm_gain, w_out_att, w_out_ssm, kv_cache, ssm_state,
):
    R, piece = residual.shape
    MR = R // B
    width = piece * H
    cq, ckv, cx = w_query.shape[1], w_keyval.shape[1], w_ssm_x.shape[1]
    wr = w_write_read.shape[1]
    NS = wr // 2
    cw = wr // H if (wr // H) % 128 == 0 else wr
    qw = cq + cw if cw != wr else cq
    cols = cq + ckv + cw + 2 * cx
    hl = w_dt.shape[1]
    gl = cq // HD
    heads_all = gl * H
    wide = -(-(piece + 3) // 128) * 128
    st = ssm_state.reshape(MR, hl * ssm_state.shape[2], NS)
    vm = pl.BlockSpec(memory_space=pltpu.VMEM)
    hbm = pl.BlockSpec(memory_space=pltpu.HBM)
    dma = pltpu.SemaphoreType.DMA
    V = pltpu.VMEM
    scratch = [
        V(w_query.shape, BF16), V(w_keyval.shape, BF16), V(w_ssm_x.shape, BF16), V(w_ssm_z.shape, BF16),
        V((w_write_read.shape[0], cw), BF16), V((hl, w_dt.shape[0]), BF16), V(w_out_att.shape, BF16), V(w_out_ssm.shape, BF16),
        V(kv_cache.shape, BF16),
        V((R, piece), BF16), V((1, R), jnp.int32), V(norm_gain.shape, BF16), V((1, R), jnp.int32),
        V((1, hl), F32), V((1, hl), F32), V((1, hl), F32), V((1, cx), F32),
        V((H, R, wide), BF16), V((R, width), BF16),
        V((B, MR, cols), BF16), V((B, MR, cols), BF16), V((R, cols), F32), V((R, HD), F32), V((B, MR, HD), F32),
        V((H, MR, qw), BF16), V((H, MR, ckv), BF16),
        V((heads_all * MR, HD), F32), V((MR, ckv * H), F32), V((MR, wr), F32), V((MR, HD), F32), V((R, piece), F32),
        V((cx, 3 * MR), F32), V((2 * MR, MR * NS), BF16),
        V((H, MR, gl, HD), F32), V((H, MR, gl, HD), F32), V((H, gl, HD), F32), V((H, gl, HD), F32),
        V((MR, HD), F32), V((H, MR, HD), F32), V((gl * MR, HD), F32),
        V((B, MR, cx), BF16), V((B, MR, cq), BF16), V((B, MR, HD), F32),
        V((H, R, piece), BF16), V((H, R, piece), BF16),
        dma((9,)), dma((7,)), dma((MR,)), dma((MR,)), dma((2, 1, H)), dma((2, 5, B)), dma((2, 2, H)),
        dma((2, PARTS + 2, H)), dma((2, 3, B)), dma((2, 1, H)),
    ]

    def near(*arrays):
        return [pltpu.with_memory_space_constraint(a, pltpu.VMEM) for a in arrays]

    def far(*arrays):
        return [pltpu.with_memory_space_constraint(a, pltpu.HBM) for a in arrays]

    out_res, new_state = pl.pallas_call(
        functools.partial(mixer_kernel, (B, H, MR, NS)),
        out_shape=(V((R, piece), BF16), V(st.shape, F32)),
        in_specs=[hbm] * 18,
        out_specs=(vm, vm),
        scratch_shapes=scratch,
        compiler_params=pltpu.CompilerParams(collective_id=0, has_side_effects=True, vmem_limit_bytes=50 * MIB),
        name="mixer",
    )(*far(
        residual, arrival.reshape(1, R), lengths.reshape(1, R), norm_gain,
        dt_bias.reshape(1, hl), a_rate.reshape(1, hl), skip_gain.reshape(1, hl), ssm_gain.reshape(1, cx), w_dt.T,
        w_query, w_keyval, w_ssm_x, w_ssm_z, w_write_read, w_out_att, w_out_ssm, kv_cache, st,
    ))
    out_res, new_state = pl.pallas_call(
        deliver_kernel,
        out_shape=(jax.ShapeDtypeStruct((R, piece), BF16), jax.ShapeDtypeStruct(st.shape, F32)),
        in_specs=[vm, vm],
        out_specs=(hbm, hbm),
        scratch_shapes=[dma((MR + 1,))],
        compiler_params=pltpu.CompilerParams(vmem_limit_bytes=16 * MIB),
        name="deliver",
    )(*near(out_res, new_state))
    return (out_res, new_state.reshape(ssm_state.shape))


def solution(mesh):
    return jax.shard_map(
        functools.partial(body, mesh.shape["branch"], mesh.shape["heads"]),
        mesh=mesh,
        in_specs=(
            P("parts", ("branch", "heads")),
            P("parts"),
            P("parts"),
            P(("branch", "heads")),
            P("branch", "heads"),
            P("branch", "heads"),
            P("branch", "heads"),
            P("branch", "heads"),
            P("branch", None),
            P("branch", "heads"),
            P("heads"),
            P("heads"),
            P("heads"),
            P("heads"),
            P("heads", "branch"),
            P("heads", "branch"),
            P(("parts", "branch"), "heads", None),
            P(("parts", "branch"), "heads", None, None),
        ),
        out_specs=(P("parts", ("branch", "heads")), P(("parts", "branch"), "heads", None, None)),
        check_vma=False,
    )
```

```python
import functools

import jax
import jax.numpy as jnp
from jax import lax
from jax.experimental import pallas as pl
from jax.experimental.pallas import tpu as pltpu
from jax.sharding import PartitionSpec as P

HD = 128
NEG = -1e30
PARTS = 2
F32 = jnp.float32
BF16 = jnp.bfloat16
MIB = 1024 * 1024
NT = (((1,), (1,)), ((), ()))
TN = (((0,), (0,)), ((), ()))
MESH = pl.DeviceIdType.MESH


def dot(a, b):
    return jnp.dot(a, b, preferred_element_type=F32)


def iota(shape, dim):
    return lax.broadcasted_iota(jnp.int32, shape, dim)


def split3(v):
    a = v.astype(BF16).astype(F32)
    c = (v - a).astype(BF16).astype(F32)
    return a, c, v - a - c


def lanes(n):
    return -(-n // HD) * HD


class Links:
    def __init__(self, B, H):
        self.n = {"heads": H, "branch": B}
        self.me = {"heads": lax.axis_index("heads"), "branch": lax.axis_index("branch")}
        self.pending = []

    def to(self, axis, d):
        n, me = self.n[axis], self.me[axis]
        if axis == "heads" and n % 2 == 0:
            return lax.rem(me // 2 + d // 2, n // 2) * 2 + lax.rem(me + d % 2, 2)
        return lax.rem(me + d, n)

    def order(self, axis):
        n = self.n[axis]
        if axis == "heads":
            return list(range(n - 1, 0, -1))
        return sorted(range(1, n), key=lambda d: (-min(d, n - d), d))

    def greet(self):
        barrier = pltpu.get_barrier_semaphore()
        for axis in ("branch", "heads"):
            for d in self.order(axis):
                pl.semaphore_signal(barrier, 1, device_id={axis: self.to(axis, d)}, device_id_type=MESH)

    def greeted(self):
        pl.semaphore_wait(pltpu.get_barrier_semaphore(), self.n["heads"] + self.n["branch"] - 2)

    def push(self, src, dst, sems, k, axis, d):
        c = pltpu.make_async_remote_copy(
            src_ref=src, dst_ref=dst, send_sem=sems.at[0, k, d], recv_sem=sems.at[1, k, d],
            device_id={axis: self.to(axis, d)}, device_id_type=MESH,
        )
        c.start()
        self.pending.append(c)
        return c

    def drain(self):
        for c in self.pending:
            c.wait_send()
        self.pending = []


def attender(H, MR, h, q2, kvn, len_v, kv_v, keep):
    heads_all = q2.shape[0] // MR
    kw = kvn.shape[1] // 2
    kvh = kw // HD
    span = kv_v.shape[1]
    block_mask = iota((heads_all, kw), 0) // (heads_all // kvh) == iota((heads_all, kw), 1) // HD
    lane = iota((heads_all, HD), 1)
    pos = (h * span + iota((heads_all, span), 1)).astype(F32)
    scaling = HD ** (-0.5)
    is_first = h == 0

    def attend(r, mz):
        q = q2[pl.ds(r, heads_all, stride=MR), :]
        qb = jnp.where(block_mask, jnp.concatenate([q] * kvh, axis=1), 0.0)
        scores = lax.dot_general(qb.astype(BF16), kv_v[r, :, 0:kw], NT, preferred_element_type=F32) * scaling
        valid = pos < jnp.concatenate([len_v[pl.ds(r, 1), :]] * (span // HD), axis=1)
        scores = jnp.where(valid, scores, NEG)
        s_new = jnp.sum(qb * kvn[pl.ds(r, 1), 0:kw], axis=1, keepdims=True) * scaling
        top = jnp.maximum(jnp.max(scores, axis=1, keepdims=True), jnp.where(is_first, s_new, NEG))
        probs = jnp.where(valid, jnp.exp(scores - top), 0.0).astype(BF16)
        p_new = jnp.where(is_first, jnp.exp(s_new - top), 0.0).astype(BF16).astype(F32)
        z = jnp.sum(probs.astype(F32), axis=1, keepdims=True) + p_new
        o = dot(probs, kv_v[r, :, kw:2 * kw])
        o = jnp.where(block_mask, o + p_new * kvn[pl.ds(r, 1), kw:2 * kw], 0.0)
        acc = o[:, 0:HD]
        for e in range(1, kvh):
            acc = acc + o[:, e * HD:(e + 1) * HD]
        gl = heads_all // H
        for i in range(H):
            keep[i, r] = acc[i * gl:(i + 1) * gl]
        return jnp.where(lane == r, top, jnp.where(lane == MR + r, z, mz))

    return attend


def mixer_kernel(
    cfg,
    res, arr_row, lens, gain, dt_bias, a_rate, skip, ssm_gain, w_dt,
    w_q, w_kv, w_x, w_z, w_wr, w_oa, w_os, kv, st,
    out_res, st_v,
    wq_v, wkv_v, wx_v, wz_v, wwr_v, wdt_v, woa_v, wos_v, kv_v,
    res_v, arr_v, gain_v, lens_v, bias_v, rate_v, skip_v, sg_v,
    xin, xg, sb, rb, own, qg, kvg, q2, kvn, wrn, len_v, ord_v, cols_v, wm,
    accs, accr, gss, gsr, at2, ge, ga, fs, fr,
    ssem, wsem, kvsem, stsem, asem, bsem, csem, dsem, esem, fsem,
):
    B, H, MR, NS = cfg
    R = B * MR
    links = Links(B, H)
    b, h = links.me["branch"], links.me["heads"]
    piece = res.shape[1]
    model = piece * H * B
    cq, ckv, cx, cz, cw = (w_q.shape[1], w_kv.shape[1], w_x.shape[1], w_z.shape[1], wwr_v.shape[1])
    o_sum = cq
    o_kv = o_sum + HD
    o_wr = o_kv + ckv
    o_dt = o_wr + cw
    hl = w_dt.shape[0]
    o_x = o_dt + lanes(3 * hl)
    o_z = o_x + cx
    total_cols = o_z + cz
    sp = cx // hl
    heads_all = cq * H // HD
    gl = cq // HD

    links.greet()
    small = [
        pltpu.make_async_copy(src, dst, ssem.at[i])
        for i, (src, dst) in enumerate((
            (res, res_v), (arr_row, arr_v), (gain, gain_v), (lens, lens_v), (dt_bias, bias_v), (a_rate, rate_v),
            (skip, skip_v), (ssm_gain, sg_v), (w_dt, wdt_v),
        ))
    ]
    for c in small[:3]:
        c.start()
    weights = [
        pltpu.make_async_copy(src, dst, wsem.at[i])
        for i, (src, dst) in enumerate(((w_q, wq_v), (w_kv, wkv_v), (w_wr, wwr_v), (w_x, wx_v), (w_z, wz_v), (w_os, wos_v), (w_oa, woa_v)))
    ]
    for c in weights[:2] + small[3:] + weights[2:5]:
        c.start()
    for c in small[:3]:
        c.wait()

    perm = (iota((R, R), 0) == arr_v[...]).astype(BF16)
    rows = dot(perm, res_v[...])
    ord_v[...] = rows
    wide = xin.shape[2]
    sums = split3(jnp.sum(rows * rows, axis=1, keepdims=True))
    tail = jnp.zeros((R, wide - piece), F32)
    for i, part in enumerate(sums):
        tail = jnp.where(iota(tail.shape, 1) == i, part, tail)
    xin[0, :, 0:piece] = (rows * gain_v[...].reshape(1, piece).astype(F32)).astype(BF16)
    xin[0, :, piece:wide] = tail.astype(BF16)

    links.greeted()
    got = [links.push(xin.at[0], xin.at[d], asem, 0, "heads", d) for d in links.order("heads")]
    state_in = [pltpu.make_async_copy(st.at[r], st_v.at[r], stsem.at[r]) for r in range(MR)]
    cache_in = [pltpu.make_async_copy(kv.at[r], kv_v.at[r], kvsem.at[r]) for r in range(MR)]
    for c in state_in + cache_in + weights[5:]:
        c.start()
    for c in small[3:]:
        c.wait()
    mine = (iota((MR, R), 1) == b * MR + iota((MR, R), 0)).astype(F32)
    len_v[...] = jnp.broadcast_to(jnp.sum(mine * lens_v[...].astype(F32), axis=1, keepdims=True), (MR, HD))
    for c in got:
        c.wait_recv()

    def slot(i):
        if H % 2 == 0:
            dx = lax.rem(h // 2 - i // 2 + H // 2, H // 2)
            dc = lax.rem(h - i % 2 + 2, 2)
            return dx * 2 + dc
        return lax.rem(h - i + H, H)

    sumsq = jnp.zeros((R, 1), F32)
    for i in range(H):
        part = xin[slot(i)]
        xg[:, i * piece:(i + 1) * piece] = part[:, 0:piece]
        t = part[:, piece:wide].astype(F32)
        sumsq = sumsq + jnp.sum(jnp.where(iota(t.shape, 1) < 3, t, 0.0), axis=1, keepdims=True)
    x = xg[...]

    def project(i, w_ref, lo, hi):
        weights[i].wait()
        val = dot(x, w_ref[...])
        own[:, lo:hi] = val
        for j in range(B):
            sb[j, :, lo:hi] = val[j * MR:(j + 1) * MR].astype(BF16)

    def scatter(k, lo, hi):
        return [
            links.push(sb.at[lax.rem(b + d, B), :, lo:hi], rb.at[d, :, lo:hi], bsem, k, "branch", d)
            for d in links.order("branch")
        ]

    def spread3(v, lo, hi):
        n = v.shape[1]
        val = jnp.zeros((R, hi - lo), F32)
        for i, part in enumerate(split3(v)):
            if n == 1:
                val = jnp.where(iota(val.shape, 1) == i, part, val)
            else:
                val = val + dot(part.astype(BF16), (iota((n, hi - lo), 1) == iota((n, hi - lo), 0) + i * n).astype(BF16))
        own[:, lo:hi] = val
        for j in range(B):
            sb[j, :, lo:hi] = val[j * MR:(j + 1) * MR].astype(BF16)

    spread3(sumsq, o_sum, o_kv)
    project(0, wq_v, 0, cq)
    got_q = scatter(0, 0, o_kv)
    project(1, wkv_v, o_kv, o_wr)
    got_kv = scatter(1, o_kv, o_wr)
    project(2, wwr_v, o_wr, o_dt)
    spread3(lax.dot_general(x, wdt_v[...], NT, preferred_element_type=F32), o_dt, o_x)
    got_wr = scatter(2, o_wr, o_x)
    project(3, wx_v, o_x, o_z)
    project(4, wz_v, o_z, total_cols)
    my_rows = pl.ds(pl.multiple_of(b * MR, MR), MR)
    for c in got_q:
        c.wait_recv()

    def gathered(lo, hi):
        val = own[my_rows, lo:hi]
        for d in range(1, B):
            val = val + rb[d, :, lo:hi].astype(F32)
        return val

    scale = lax.rsqrt(jnp.sum(gathered(o_sum, o_kv)[:, 0:3], axis=1, keepdims=True) / model + 1e-05)

    def reduced(lo, hi):
        return (gathered(lo, hi) * scale).astype(BF16)

    qg[h] = reduced(0, cq)
    got_a = [links.push(qg.at[h], qg.at[h], csem, 0, "heads", d) for d in links.order("heads")]
    for c in got_kv:
        c.wait_recv()
    kvg[h] = reduced(o_kv, o_wr)
    got_b = [links.push(kvg.at[h], kvg.at[h], csem, 1, "heads", d) for d in links.order("heads")]
    got_xz = scatter(3, o_x, total_cols)
    for c in got_wr:
        c.wait_recv()
    wrn[...] = reduced(o_wr, o_dt).astype(F32)
    write = wrn[:, 0:NS]
    read = wrn[:, NS:2 * NS]
    read_b = read.astype(BF16)
    row = iota((MR, cx), 0)
    for c in state_in:
        c.wait()

    def readout(r, y):
        part = lax.dot_general(read_b, st_v[r].astype(BF16), NT, preferred_element_type=F32)
        return jnp.where(row == r, part, y)

    y = lax.fori_loop(0, MR, readout, jnp.zeros((MR, cx), F32), unroll=2)
    dt_sum = gathered(o_dt, o_x)
    dt_raw = (dt_sum[:, 0:hl] + dt_sum[:, hl:2 * hl]) + dt_sum[:, 2 * hl:3 * hl]
    pre = dt_raw * scale + bias_v[...]
    step = jnp.maximum(pre, 0.0) + jnp.log1p(jnp.exp(-jnp.abs(pre)))
    decay = jnp.exp(-step * rate_v[...])
    spread = (iota((hl, cx), 1) // sp == iota((hl, cx), 0)).astype(F32)

    def widen(v):
        return jnp.dot(v, spread, preferred_element_type=F32, precision=lax.Precision.HIGHEST)

    decay_w = widen(decay)
    step_w = widen(step)
    skip_w = widen(jnp.broadcast_to(skip_v[...], (MR, hl)))
    for c in got_a:
        c.wait_recv()
    for g in range(heads_all):
        q2[g * MR:(g + 1) * MR, :] = qg[g // gl, :, (g % gl) * HD:(g % gl + 1) * HD].astype(F32)
    for c in got_b:
        c.wait_recv()
    for i in range(H):
        kvn[:, i * ckv:(i + 1) * ckv] = kvg[i].astype(F32)
    attend = attender(H, MR, h, q2, kvn, len_v, kv_v, accs)
    mz = jnp.zeros((heads_all, HD), F32)
    got = []
    for k in range(PARTS):
        lo, hi = k * MR // PARTS, (k + 1) * MR // PARTS
        for r in range(lo, hi):
            cache_in[r].wait()
        for r in range(lo, hi):
            mz = attend(r, mz)
        end = hi
        if hi == MR:
            end = MR + 1
            for i in range(H):
                accs[i, MR] = mz[i * gl:(i + 1) * gl]
        for d in links.order("heads"):
            got.append(links.push(accs.at[links.to("heads", d), lo:end], accr.at[d, lo:end], dsem, k, "heads", d))
        if k == 0:
            for c in got_xz:
                c.wait_recv()
            ssm_x = reduced(o_x, o_z).astype(F32)
            ssm_z = reduced(o_z, total_cols).astype(F32)
            dtx = step_w * ssm_x
            y = decay_w * y + dtx * jnp.sum(write * read, axis=1, keepdims=True) + skip_w * ssm_x
            gated = y * (ssm_z * jax.nn.sigmoid(ssm_z))
            own_gate = jnp.broadcast_to(jnp.sum(gated * gated, axis=1, keepdims=True), (MR, HD))
            gss[...] = own_gate
            got_gate = [links.push(gss, gsr.at[d], dsem, PARTS, "heads", d) for d in links.order("heads")]
    for c in got_gate:
        c.wait_recv()
    gate = own_gate
    for d in range(1, H):
        gate = gate + gsr[d]
    ge[b] = (gated * lax.rsqrt(gate[:, 0:1] / (cx * H) + 1e-05) * sg_v[...]).astype(BF16)
    got_e = [links.push(ge.at[b], ge.at[b], esem, 0, "branch", d) for d in links.order("branch")]
    dtx_hi = dtx.astype(BF16).astype(F32)
    cols_v[...] = jnp.transpose(jnp.concatenate([dtx_hi, dtx - dtx_hi, decay_w], axis=0))
    turn = lax.rem(iota((2 * MR, NS), 0), MR)
    for r in range(MR):
        wm[:, r * NS:(r + 1) * NS] = jnp.where(turn == r, wrn[r:r + 1, 0:NS], 0.0).astype(BF16)
    def renew(i, carry):
        at = pl.multiple_of(i * sp, sp)
        lhs = cols_v[pl.ds(at, sp), 0:2 * MR].astype(BF16)
        keep = cols_v[pl.ds(at, 1), :]
        for r in range(MR):
            st_v[r, pl.ds(at, sp), :] = (
                keep[:, 2 * MR + r:2 * MR + r + 1] * st_v[r, pl.ds(at, sp), :] + dot(lhs, wm[:, r * NS:(r + 1) * NS])
            )
        return carry

    cut = hl // 2
    lax.fori_loop(0, cut, renew, 0, unroll=4 if cut % 4 == 0 else 1)
    for c in got:
        c.wait_recv()
    accr[0] = accs[h]
    mzr = [accr[i, MR] for i in range(H)]
    for r in range(MR):
        tops = [mzr[i][:, r:r + 1] for i in range(H)]
        best = functools.reduce(jnp.maximum, tops)
        num = jnp.zeros((gl, HD), F32)
        den = jnp.zeros((gl, 1), F32)
        for i in range(H):
            f = jnp.exp(tops[i] - best)
            num = num + f * accr[i, r]
            den = den + f * mzr[i][:, MR + r:MR + r + 1]
        at2[pl.ds(r, gl, stride=MR), :] = num / den
    for g in range(gl):
        ga[b, :, g * HD:(g + 1) * HD] = at2[g * MR:(g + 1) * MR, :].astype(BF16)
    got_a = [links.push(ga.at[b], ga.at[b], esem, 1, "branch", d) for d in links.order("branch")]
    def stacked(ref):
        return jnp.concatenate([ref[i].astype(F32) for i in range(B)], axis=0)

    lax.fori_loop(cut, hl, renew, 0, unroll=4 if (hl - cut) % 4 == 0 else 1)
    for c in weights[5:]:
        c.wait()
    for c in got_e:
        c.wait_recv()
    ssm_part = dot(stacked(ge).astype(BF16), wos_v[...])
    links.drain()
    for c in got_a:
        c.wait_recv()
    part = dot(stacked(ga).astype(BF16), woa_v[...]) + ssm_part
    for i in range(H):
        fs[i] = part[:, i * piece:(i + 1) * piece].astype(fs.dtype)
    got = [links.push(fs.at[links.to("heads", d)], fr.at[d], fsem, 0, "heads", d) for d in links.order("heads")]
    total = ord_v[...] + fs[h].astype(F32)
    for c in got:
        c.wait_recv()
    for d in range(1, H):
        total = total + fr[d].astype(F32)
    out_res[...] = lax.dot_general(perm, total.astype(BF16), TN, preferred_element_type=F32).astype(BF16)
    links.drain()


def deliver_kernel(res, st, out_res, out_st, sem):
    copies = [pltpu.make_async_copy(res, out_res, sem.at[0])]
    for r in range(st.shape[0]):
        copies.append(pltpu.make_async_copy(st.at[r], out_st.at[r], sem.at[r + 1]))
    for c in copies:
        c.start()
    for c in copies:
        c.wait()


def body(
    B, H,
    residual, arrival, lengths, norm_gain, w_query, w_keyval, w_ssm_x, w_ssm_z, w_write_read, w_dt,
    dt_bias, a_rate, skip_gain, ssm_gain, w_out_att, w_out_ssm, kv_cache, ssm_state,
):
    R, piece = residual.shape
    MR = R // B
    width = piece * H
    cq, ckv, cx = w_query.shape[1], w_keyval.shape[1], w_ssm_x.shape[1]
    wr = w_write_read.shape[1]
    NS = wr // 2
    hl = w_dt.shape[1]
    cols = cq + wr + HD + ckv + 2 * cx + lanes(3 * hl)
    gl = cq // HD
    heads_all = gl * H
    wide = -(-(piece + 3) // 128) * 128
    st = ssm_state.reshape(MR, hl * ssm_state.shape[2], NS)
    vm = pl.BlockSpec(memory_space=pltpu.VMEM)
    hbm = pl.BlockSpec(memory_space=pltpu.HBM)
    dma = pltpu.SemaphoreType.DMA
    V = pltpu.VMEM
    scratch = [
        V(w_query.shape, BF16), V(w_keyval.shape, BF16), V(w_ssm_x.shape, BF16), V(w_ssm_z.shape, BF16),
        V(w_write_read.shape, BF16), V((hl, w_dt.shape[0]), BF16), V(w_out_att.shape, BF16), V(w_out_ssm.shape, BF16),
        V(kv_cache.shape, BF16),
        V((R, piece), BF16), V((1, R), jnp.int32), V(norm_gain.shape, BF16), V((1, R), jnp.int32),
        V((1, hl), F32), V((1, hl), F32), V((1, hl), F32), V((1, cx), F32),
        V((H, R, wide), BF16), V((R, width), BF16),
        V((B, MR, cols), BF16), V((B, MR, cols), BF16), V((R, cols), F32),
        V((H, MR, cq), BF16), V((H, MR, ckv), BF16),
        V((heads_all * MR, HD), F32), V((MR, ckv * H), F32), V((MR, wr), F32), V((MR, HD), F32), V((R, piece), F32),
        V((cx, 3 * MR), F32), V((2 * MR, MR * NS), BF16),
        V((H, MR + 1, gl, HD), F32), V((H, MR + 1, gl, HD), F32),
        V((MR, HD), F32), V((H, MR, HD), F32), V((gl * MR, HD), F32),
        V((B, MR, cx), BF16), V((B, MR, cq), BF16),
        V((H, R, piece), BF16), V((H, R, piece), BF16),
        dma((9,)), dma((7,)), dma((MR,)), dma((MR,)), dma((2, 1, H)), dma((2, 4, B)), dma((2, 2, H)),
        dma((2, PARTS + 1, H)), dma((2, 2, B)), dma((2, 1, H)),
    ]

    def near(*arrays):
        return [pltpu.with_memory_space_constraint(a, pltpu.VMEM) for a in arrays]

    def far(*arrays):
        return [pltpu.with_memory_space_constraint(a, pltpu.HBM) for a in arrays]

    out_res, new_state = pl.pallas_call(
        functools.partial(mixer_kernel, (B, H, MR, NS)),
        out_shape=(V((R, piece), BF16), V(st.shape, F32)),
        in_specs=[hbm] * 18,
        out_specs=(vm, vm),
        scratch_shapes=scratch,
        compiler_params=pltpu.CompilerParams(collective_id=0, has_side_effects=True, vmem_limit_bytes=50 * MIB),
        name="mixer",
    )(*far(
        residual, arrival.reshape(1, R), lengths.reshape(1, R), norm_gain,
        dt_bias.reshape(1, hl), a_rate.reshape(1, hl), skip_gain.reshape(1, hl), ssm_gain.reshape(1, cx), w_dt.T,
        w_query, w_keyval, w_ssm_x, w_ssm_z, w_write_read, w_out_att, w_out_ssm, kv_cache, st,
    ))
    out_res, new_state = pl.pallas_call(
        deliver_kernel,
        out_shape=(jax.ShapeDtypeStruct((R, piece), BF16), jax.ShapeDtypeStruct(st.shape, F32)),
        in_specs=[vm, vm],
        out_specs=(hbm, hbm),
        scratch_shapes=[dma((MR + 1,))],
        compiler_params=pltpu.CompilerParams(vmem_limit_bytes=16 * MIB),
        name="deliver",
    )(*near(out_res, new_state))
    return (out_res, new_state.reshape(ssm_state.shape))


def solution(mesh):
    return jax.shard_map(
        functools.partial(body, mesh.shape["branch"], mesh.shape["heads"]),
        mesh=mesh,
        in_specs=(
            P("parts", ("branch", "heads")),
            P("parts"),
            P("parts"),
            P(("branch", "heads")),
            P("branch", "heads"),
            P("branch", "heads"),
            P("branch", "heads"),
            P("branch", "heads"),
            P("branch", None),
            P("branch", "heads"),
            P("heads"),
            P("heads"),
            P("heads"),
            P("heads"),
            P("heads", "branch"),
            P("heads", "branch"),
            P(("parts", "branch"), "heads", None),
            P(("parts", "branch"), "heads", None, None),
        ),
        out_specs=(P("parts", ("branch", "heads")), P(("parts", "branch"), "heads", None, None)),
        check_vma=False,
    )
```

```python
import functools

import jax
import jax.numpy as jnp
from jax import lax
from jax.experimental import pallas as pl
from jax.experimental.pallas import tpu as pltpu
from jax.sharding import PartitionSpec as P

HD = 128
NEG = -1e30
PARTS = 2
F32 = jnp.float32
BF16 = jnp.bfloat16
MIB = 1024 * 1024
NT = (((1,), (1,)), ((), ()))
TN = (((0,), (0,)), ((), ()))
MESH = pl.DeviceIdType.MESH


def dot(a, b):
    return jnp.dot(a, b, preferred_element_type=F32)


def iota(shape, dim):
    return lax.broadcasted_iota(jnp.int32, shape, dim)


def split3(v):
    a = v.astype(BF16).astype(F32)
    c = (v - a).astype(BF16).astype(F32)
    return a, c, v - a - c


def lanes(n):
    return -(-n // HD) * HD


class Links:
    def __init__(self, B, H):
        self.n = {"heads": H, "branch": B}
        self.me = {"heads": lax.axis_index("heads"), "branch": lax.axis_index("branch")}
        self.pending = []

    def to(self, axis, d):
        n, me = self.n[axis], self.me[axis]
        if axis == "heads" and n % 2 == 0:
            return lax.rem(me // 2 + d // 2, n // 2) * 2 + lax.rem(me + d % 2, 2)
        return lax.rem(me + d, n)

    def order(self, axis):
        n = self.n[axis]
        if axis == "heads":
            return list(range(n - 1, 0, -1))
        return sorted(range(1, n), key=lambda d: (-min(d, n - d), d))

    def greet(self):
        barrier = pltpu.get_barrier_semaphore()
        for axis in ("branch", "heads"):
            for d in self.order(axis):
                pl.semaphore_signal(barrier, 1, device_id={axis: self.to(axis, d)}, device_id_type=MESH)

    def greeted(self):
        pl.semaphore_wait(pltpu.get_barrier_semaphore(), self.n["heads"] + self.n["branch"] - 2)

    def push(self, src, dst, sems, k, axis, d):
        c = pltpu.make_async_remote_copy(
            src_ref=src, dst_ref=dst, send_sem=sems.at[0, k, d], recv_sem=sems.at[1, k, d],
            device_id={axis: self.to(axis, d)}, device_id_type=MESH,
        )
        c.start()
        self.pending.append(c)
        return c

    def drain(self):
        for c in self.pending:
            c.wait_send()
        self.pending = []


def attender(H, MR, h, q2, kvn, len_v, kv_v, keep):
    heads_all = q2.shape[0] // MR
    kw = kvn.shape[1] // 2
    kvh = kw // HD
    span = kv_v.shape[1]
    block_mask = iota((heads_all, kw), 0) // (heads_all // kvh) == iota((heads_all, kw), 1) // HD
    lane = iota((heads_all, HD), 1)
    pos = (h * span + iota((heads_all, span), 1)).astype(F32)
    scaling = HD ** (-0.5)
    is_first = h == 0

    def attend(r, mz):
        q = q2[pl.ds(r, heads_all, stride=MR), :]
        qb = jnp.where(block_mask, jnp.concatenate([q] * kvh, axis=1), 0.0)
        scores = lax.dot_general(qb.astype(BF16), kv_v[r, :, 0:kw], NT, preferred_element_type=F32) * scaling
        valid = pos < jnp.concatenate([len_v[pl.ds(r, 1), :]] * (span // HD), axis=1)
        scores = jnp.where(valid, scores, NEG)
        s_new = jnp.sum(qb * kvn[pl.ds(r, 1), 0:kw], axis=1, keepdims=True) * scaling
        top = jnp.maximum(jnp.max(scores, axis=1, keepdims=True), jnp.where(is_first, s_new, NEG))
        probs = jnp.where(valid, jnp.exp(scores - top), 0.0).astype(BF16)
        p_new = jnp.where(is_first, jnp.exp(s_new - top), 0.0).astype(BF16).astype(F32)
        z = jnp.sum(probs.astype(F32), axis=1, keepdims=True) + p_new
        o = dot(probs, kv_v[r, :, kw:2 * kw])
        o = jnp.where(block_mask, o + p_new * kvn[pl.ds(r, 1), kw:2 * kw], 0.0)
        acc = o[:, 0:HD]
        for e in range(1, kvh):
            acc = acc + o[:, e * HD:(e + 1) * HD]
        gl = heads_all // H
        for i in range(H):
            keep[i, r] = acc[i * gl:(i + 1) * gl]
        return jnp.where(lane == r, top, jnp.where(lane == MR + r, z, mz))

    return attend


def mixer_kernel(
    cfg,
    res, arr_row, lens, gain, dt_bias, a_rate, skip, ssm_gain, w_dt,
    w_q, w_kv, w_x, w_z, w_wr, w_oa, w_os, kv, st,
    out_res, st_v,
    wq_v, wkv_v, wx_v, wz_v, wwr_v, wdt_v, woa_v, wos_v, kv_v,
    res_v, arr_v, gain_v, lens_v, bias_v, rate_v, skip_v, sg_v,
    xin, xg, sb, rb, own, qg, kvg, q2, kvn, wrn, len_v, ord_v, cols_v, wm,
    accs, accr, gss, gsr, at2, ge, ga, ssm_v, fs, fr,
    ssem, wsem, kvsem, stsem, asem, bsem, csem, dsem, esem, fsem,
):
    B, H, MR, NS = cfg
    R = B * MR
    links = Links(B, H)
    b, h = links.me["branch"], links.me["heads"]
    piece = res.shape[1]
    model = piece * H * B
    cq, ckv, cx, cz, cw = (w_q.shape[1], w_kv.shape[1], w_x.shape[1], w_z.shape[1], wwr_v.shape[1])
    o_sum = cq
    o_kv = o_sum + HD
    o_wr = o_kv + ckv
    o_dt = o_wr + cw
    hl = w_dt.shape[0]
    o_x = o_dt + lanes(3 * hl)
    o_z = o_x + cx
    total_cols = o_z + cz
    sp = cx // hl
    heads_all = cq * H // HD
    gl = cq // HD

    links.greet()
    small = [
        pltpu.make_async_copy(src, dst, ssem.at[i])
        for i, (src, dst) in enumerate((
            (res, res_v), (arr_row, arr_v), (gain, gain_v), (lens, lens_v), (dt_bias, bias_v), (a_rate, rate_v),
            (skip, skip_v), (ssm_gain, sg_v), (w_dt, wdt_v),
        ))
    ]
    for c in small[:3]:
        c.start()
    weights = [
        pltpu.make_async_copy(src, dst, wsem.at[i])
        for i, (src, dst) in enumerate(((w_q, wq_v), (w_kv, wkv_v), (w_wr, wwr_v), (w_x, wx_v), (w_z, wz_v), (w_os, wos_v), (w_oa, woa_v)))
    ]
    for c in weights[:2] + small[3:] + weights[2:5]:
        c.start()
    for c in small[:3]:
        c.wait()

    perm = (iota((R, R), 0) == arr_v[...]).astype(BF16)
    rows = dot(perm, res_v[...])
    ord_v[...] = rows
    wide = xin.shape[2]
    sums = split3(jnp.sum(rows * rows, axis=1, keepdims=True))
    tail = jnp.zeros((R, wide - piece), F32)
    for i, part in enumerate(sums):
        tail = jnp.where(iota(tail.shape, 1) == i, part, tail)
    xin[0, :, 0:piece] = (rows * gain_v[...].reshape(1, piece).astype(F32)).astype(BF16)
    xin[0, :, piece:wide] = tail.astype(BF16)

    links.greeted()
    got = [links.push(xin.at[0], xin.at[d], asem, 0, "heads", d) for d in links.order("heads")]
    state_in = [pltpu.make_async_copy(st.at[r], st_v.at[r], stsem.at[r]) for r in range(MR)]
    cache_in = [pltpu.make_async_copy(kv.at[r], kv_v.at[r], kvsem.at[r]) for r in range(MR)]
    for c in state_in + cache_in + weights[5:]:
        c.start()
    for c in small[3:]:
        c.wait()
    mine = (iota((MR, R), 1) == b * MR + iota((MR, R), 0)).astype(F32)
    len_v[...] = jnp.broadcast_to(jnp.sum(mine * lens_v[...].astype(F32), axis=1, keepdims=True), (MR, HD))
    for c in got:
        c.wait_recv()

    def slot(i):
        if H % 2 == 0:
            dx = lax.rem(h // 2 - i // 2 + H // 2, H // 2)
            dc = lax.rem(h - i % 2 + 2, 2)
            return dx * 2 + dc
        return lax.rem(h - i + H, H)

    sumsq = jnp.zeros((R, 1), F32)
    for i in range(H):
        part = xin[slot(i)]
        xg[:, i * piece:(i + 1) * piece] = part[:, 0:piece]
        t = part[:, piece:wide].astype(F32)
        sumsq = sumsq + jnp.sum(jnp.where(iota(t.shape, 1) < 3, t, 0.0), axis=1, keepdims=True)
    x = xg[...]

    def project(i, w_ref, lo, hi):
        weights[i].wait()
        val = dot(x, w_ref[...])
        own[:, lo:hi] = val
        for j in range(B):
            sb[j, :, lo:hi] = val[j * MR:(j + 1) * MR].astype(BF16)

    def scatter(k, lo, hi):
        return [
            links.push(sb.at[lax.rem(b + d, B), :, lo:hi], rb.at[d, :, lo:hi], bsem, k, "branch", d)
            for d in links.order("branch")
        ]

    def spread3(v, lo, hi):
        n = v.shape[1]
        val = jnp.zeros((R, hi - lo), F32)
        for i, part in enumerate(split3(v)):
            if n == 1:
                val = jnp.where(iota(val.shape, 1) == i, part, val)
            else:
                val = val + dot(part.astype(BF16), (iota((n, hi - lo), 1) == iota((n, hi - lo), 0) + i * n).astype(BF16))
        own[:, lo:hi] = val
        for j in range(B):
            sb[j, :, lo:hi] = val[j * MR:(j + 1) * MR].astype(BF16)

    spread3(sumsq, o_sum, o_kv)
    project(0, wq_v, 0, cq)
    got_q = scatter(0, 0, o_kv)
    project(1, wkv_v, o_kv, o_wr)
    got_kv = scatter(1, o_kv, o_wr)
    project(2, wwr_v, o_wr, o_dt)
    spread3(lax.dot_general(x, wdt_v[...], NT, preferred_element_type=F32), o_dt, o_x)
    got_wr = scatter(2, o_wr, o_x)
    project(3, wx_v, o_x, o_z)
    project(4, wz_v, o_z, total_cols)
    my_rows = pl.ds(pl.multiple_of(b * MR, MR), MR)
    for c in got_q:
        c.wait_recv()

    def gathered(lo, hi):
        val = own[my_rows, lo:hi]
        for d in range(1, B):
            val = val + rb[d, :, lo:hi].astype(F32)
        return val

    scale = lax.rsqrt(jnp.sum(gathered(o_sum, o_kv)[:, 0:3], axis=1, keepdims=True) / model + 1e-05)

    def reduced(lo, hi):
        return (gathered(lo, hi) * scale).astype(BF16)

    qg[h] = reduced(0, cq)
    got_a = [links.push(qg.at[h], qg.at[h], csem, 0, "heads", d) for d in links.order("heads")]
    for c in got_kv:
        c.wait_recv()
    kvg[h] = reduced(o_kv, o_wr)
    got_b = [links.push(kvg.at[h], kvg.at[h], csem, 1, "heads", d) for d in links.order("heads")]
    got_xz = scatter(3, o_x, total_cols)
    for c in got_wr:
        c.wait_recv()
    wrn[...] = reduced(o_wr, o_dt).astype(F32)
    write = wrn[:, 0:NS]
    read = wrn[:, NS:2 * NS]
    read_b = read.astype(BF16)
    row = iota((MR, cx), 0)
    for c in state_in:
        c.wait()

    def readout(r, y):
        part = lax.dot_general(read_b, st_v[r].astype(BF16), NT, preferred_element_type=F32)
        return jnp.where(row == r, part, y)

    y = lax.fori_loop(0, MR, readout, jnp.zeros((MR, cx), F32), unroll=2)
    dt_sum = gathered(o_dt, o_x)
    dt_raw = (dt_sum[:, 0:hl] + dt_sum[:, hl:2 * hl]) + dt_sum[:, 2 * hl:3 * hl]
    pre = dt_raw * scale + bias_v[...]
    step = jnp.maximum(pre, 0.0) + jnp.log1p(jnp.exp(-jnp.abs(pre)))
    decay = jnp.exp(-step * rate_v[...])
    spread = (iota((hl, cx), 1) // sp == iota((hl, cx), 0)).astype(F32)

    def widen(v):
        return jnp.dot(v, spread, preferred_element_type=F32, precision=lax.Precision.HIGHEST)

    decay_w = widen(decay)
    step_w = widen(step)
    skip_w = widen(jnp.broadcast_to(skip_v[...], (MR, hl)))
    for c in got_a:
        c.wait_recv()
    for g in range(heads_all):
        q2[g * MR:(g + 1) * MR, :] = qg[g // gl, :, (g % gl) * HD:(g % gl + 1) * HD].astype(F32)
    for c in got_b:
        c.wait_recv()
    for i in range(H):
        kvn[:, i * ckv:(i + 1) * ckv] = kvg[i].astype(F32)
    attend = attender(H, MR, h, q2, kvn, len_v, kv_v, accs)
    mz = jnp.zeros((heads_all, HD), F32)
    got = []
    first = MR - MR * 3 // 8
    for k in range(PARTS):
        lo, hi = ((0, first), (first, MR))[k]
        for r in range(lo, hi):
            cache_in[r].wait()
        for r in range(lo, hi):
            mz = attend(r, mz)
        end = hi
        if hi == MR:
            end = MR + 1
            for i in range(H):
                accs[i, MR] = mz[i * gl:(i + 1) * gl]
        for d in links.order("heads"):
            got.append(links.push(accs.at[links.to("heads", d), lo:end], accr.at[d, lo:end], dsem, k, "heads", d))
        if k == 0:
            for c in got_xz:
                c.wait_recv()
            ssm_x = reduced(o_x, o_z).astype(F32)
            ssm_z = reduced(o_z, total_cols).astype(F32)
            dtx = step_w * ssm_x
            y = decay_w * y + dtx * jnp.sum(write * read, axis=1, keepdims=True) + skip_w * ssm_x
            gated = y * (ssm_z * jax.nn.sigmoid(ssm_z))
            own_gate = jnp.broadcast_to(jnp.sum(gated * gated, axis=1, keepdims=True), (MR, HD))
            gss[...] = own_gate
            got_gate = [links.push(gss, gsr.at[d], dsem, PARTS, "heads", d) for d in links.order("heads")]
    for c in got_gate:
        c.wait_recv()
    gate = own_gate
    for d in range(1, H):
        gate = gate + gsr[d]
    ge[b] = (gated * lax.rsqrt(gate[:, 0:1] / (cx * H) + 1e-05) * sg_v[...]).astype(BF16)
    got_e = [links.push(ge.at[b], ge.at[b], esem, 0, "branch", d) for d in links.order("branch")]
    dtx_hi = dtx.astype(BF16).astype(F32)
    cols_v[...] = jnp.transpose(jnp.concatenate([dtx_hi, dtx - dtx_hi, decay_w], axis=0))
    turn = lax.rem(iota((2 * MR, NS), 0), MR)
    for r in range(MR):
        wm[:, r * NS:(r + 1) * NS] = jnp.where(turn == r, wrn[r:r + 1, 0:NS], 0.0).astype(BF16)
    def renew(i, carry):
        at = pl.multiple_of(i * sp, sp)
        lhs = cols_v[pl.ds(at, sp), 0:2 * MR].astype(BF16)
        keep = cols_v[pl.ds(at, 1), :]
        for r in range(MR):
            st_v[r, pl.ds(at, sp), :] = (
                keep[:, 2 * MR + r:2 * MR + r + 1] * st_v[r, pl.ds(at, sp), :] + dot(lhs, wm[:, r * NS:(r + 1) * NS])
            )
        return carry

    cut = hl // 2
    lax.fori_loop(0, cut, renew, 0, unroll=4 if cut % 4 == 0 else 1)
    for c in got:
        c.wait_recv()
    accr[0] = accs[h]
    mzr = [accr[i, MR] for i in range(H)]
    for r in range(MR):
        tops = [mzr[i][:, r:r + 1] for i in range(H)]
        best = functools.reduce(jnp.maximum, tops)
        num = jnp.zeros((gl, HD), F32)
        den = jnp.zeros((gl, 1), F32)
        for i in range(H):
            f = jnp.exp(tops[i] - best)
            num = num + f * accr[i, r]
            den = den + f * mzr[i][:, MR + r:MR + r + 1]
        at2[pl.ds(r, gl, stride=MR), :] = num / den
    for g in range(gl):
        ga[b, :, g * HD:(g + 1) * HD] = at2[g * MR:(g + 1) * MR, :].astype(BF16)
    got_a = [links.push(ga.at[b], ga.at[b], esem, 1, "branch", d) for d in links.order("branch")]
    def stacked(ref):
        return jnp.concatenate([ref[i].astype(F32) for i in range(B)], axis=0)

    lax.fori_loop(cut, hl, renew, 0, unroll=4 if (hl - cut) % 4 == 0 else 1)
    for c in weights[5:]:
        c.wait()
    for c in got_e:
        c.wait_recv()
    ssm_v[...] = dot(stacked(ge).astype(BF16), wos_v[...])
    links.drain()
    for c in got_a:
        c.wait_recv()
    att = stacked(ga).astype(BF16)

    def send(d):
        return links.push(fs.at[links.to("heads", d)], fr.at[d], fsem, 0, "heads", d)

    got = []
    if H % 2 == 0 and 2 * piece % HD == 0:
        for dx in list(range(1, H // 2)) + [0]:
            chip = lax.rem(h // 2 + dx, H // 2)
            at = pl.ds(pl.multiple_of(chip * 2 * piece, HD), 2 * piece)
            part = dot(att, woa_v[:, at]) + ssm_v[:, at]
            for i in range(2):
                fs[chip * 2 + i] = part[:, i * piece:(i + 1) * piece].astype(fs.dtype)
            got += [send(d) for d in (2 * dx + 1, 2 * dx) if d > 0]
    else:
        part = dot(att, woa_v[...]) + ssm_v[...]
        for i in range(H):
            fs[i] = part[:, i * piece:(i + 1) * piece].astype(fs.dtype)
        got += [send(d) for d in links.order("heads")]
    total = ord_v[...] + fs[h].astype(F32)
    for c in got:
        c.wait_recv()
    for d in range(1, H):
        total = total + fr[d].astype(F32)
    out_res[...] = lax.dot_general(perm, total.astype(BF16), TN, preferred_element_type=F32).astype(BF16)
    links.drain()


def deliver_kernel(res, st, out_res, out_st, sem):
    copies = [pltpu.make_async_copy(res, out_res, sem.at[0])]
    for r in range(st.shape[0]):
        copies.append(pltpu.make_async_copy(st.at[r], out_st.at[r], sem.at[r + 1]))
    for c in copies:
        c.start()
    for c in copies:
        c.wait()


def body(
    B, H,
    residual, arrival, lengths, norm_gain, w_query, w_keyval, w_ssm_x, w_ssm_z, w_write_read, w_dt,
    dt_bias, a_rate, skip_gain, ssm_gain, w_out_att, w_out_ssm, kv_cache, ssm_state,
):
    R, piece = residual.shape
    MR = R // B
    width = piece * H
    cq, ckv, cx = w_query.shape[1], w_keyval.shape[1], w_ssm_x.shape[1]
    wr = w_write_read.shape[1]
    NS = wr // 2
    hl = w_dt.shape[1]
    cols = cq + wr + HD + ckv + 2 * cx + lanes(3 * hl)
    gl = cq // HD
    heads_all = gl * H
    wide = -(-(piece + 3) // 128) * 128
    st = ssm_state.reshape(MR, hl * ssm_state.shape[2], NS)
    vm = pl.BlockSpec(memory_space=pltpu.VMEM)
    hbm = pl.BlockSpec(memory_space=pltpu.HBM)
    dma = pltpu.SemaphoreType.DMA
    V = pltpu.VMEM
    scratch = [
        V(w_query.shape, BF16), V(w_keyval.shape, BF16), V(w_ssm_x.shape, BF16), V(w_ssm_z.shape, BF16),
        V(w_write_read.shape, BF16), V((hl, w_dt.shape[0]), BF16), V(w_out_att.shape, BF16), V(w_out_ssm.shape, BF16),
        V(kv_cache.shape, BF16),
        V((R, piece), BF16), V((1, R), jnp.int32), V(norm_gain.shape, BF16), V((1, R), jnp.int32),
        V((1, hl), F32), V((1, hl), F32), V((1, hl), F32), V((1, cx), F32),
        V((H, R, wide), BF16), V((R, width), BF16),
        V((B, MR, cols), BF16), V((B, MR, cols), BF16), V((R, cols), F32),
        V((H, MR, cq), BF16), V((H, MR, ckv), BF16),
        V((heads_all * MR, HD), F32), V((MR, ckv * H), F32), V((MR, wr), F32), V((MR, HD), F32), V((R, piece), F32),
        V((cx, 3 * MR), F32), V((2 * MR, MR * NS), BF16),
        V((H, MR + 1, gl, HD), F32), V((H, MR + 1, gl, HD), F32),
        V((MR, HD), F32), V((H, MR, HD), F32), V((gl * MR, HD), F32),
        V((B, MR, cx), BF16), V((B, MR, cq), BF16), V((R, piece * H), F32),
        V((H, R, piece), BF16), V((H, R, piece), BF16),
        dma((9,)), dma((7,)), dma((MR,)), dma((MR,)), dma((2, 1, H)), dma((2, 4, B)), dma((2, 2, H)),
        dma((2, PARTS + 1, H)), dma((2, 2, B)), dma((2, 1, H)),
    ]

    def near(*arrays):
        return [pltpu.with_memory_space_constraint(a, pltpu.VMEM) for a in arrays]

    def far(*arrays):
        return [pltpu.with_memory_space_constraint(a, pltpu.HBM) for a in arrays]

    out_res, new_state = pl.pallas_call(
        functools.partial(mixer_kernel, (B, H, MR, NS)),
        out_shape=(V((R, piece), BF16), V(st.shape, F32)),
        in_specs=[hbm] * 18,
        out_specs=(vm, vm),
        scratch_shapes=scratch,
        compiler_params=pltpu.CompilerParams(collective_id=0, has_side_effects=True, vmem_limit_bytes=50 * MIB),
        name="mixer",
    )(*far(
        residual, arrival.reshape(1, R), lengths.reshape(1, R), norm_gain,
        dt_bias.reshape(1, hl), a_rate.reshape(1, hl), skip_gain.reshape(1, hl), ssm_gain.reshape(1, cx), w_dt.T,
        w_query, w_keyval, w_ssm_x, w_ssm_z, w_write_read, w_out_att, w_out_ssm, kv_cache, st,
    ))
    out_res, new_state = pl.pallas_call(
        deliver_kernel,
        out_shape=(jax.ShapeDtypeStruct((R, piece), BF16), jax.ShapeDtypeStruct(st.shape, F32)),
        in_specs=[vm, vm],
        out_specs=(hbm, hbm),
        scratch_shapes=[dma((MR + 1,))],
        compiler_params=pltpu.CompilerParams(vmem_limit_bytes=16 * MIB),
        name="deliver",
    )(*near(out_res, new_state))
    return (out_res, new_state.reshape(ssm_state.shape))


def solution(mesh):
    return jax.shard_map(
        functools.partial(body, mesh.shape["branch"], mesh.shape["heads"]),
        mesh=mesh,
        in_specs=(
            P("parts", ("branch", "heads")),
            P("parts"),
            P("parts"),
            P(("branch", "heads")),
            P("branch", "heads"),
            P("branch", "heads"),
            P("branch", "heads"),
            P("branch", "heads"),
            P("branch", None),
            P("branch", "heads"),
            P("heads"),
            P("heads"),
            P("heads"),
            P("heads"),
            P("heads", "branch"),
            P("heads", "branch"),
            P(("parts", "branch"), "heads", None),
            P(("parts", "branch"), "heads", None, None),
        ),
        out_specs=(P("parts", ("branch", "heads")), P(("parts", "branch"), "heads", None, None)),
        check_vma=False,
    )
```

```python
import functools

import jax
import jax.numpy as jnp
from jax import lax
from jax.experimental import pallas as pl
from jax.experimental.pallas import tpu as pltpu
from jax.sharding import PartitionSpec as P

HD = 128
NEG = -1e30
PARTS = 2
F32 = jnp.float32
BF16 = jnp.bfloat16
MIB = 1024 * 1024
NT = (((1,), (1,)), ((), ()))
TN = (((0,), (0,)), ((), ()))
MESH = pl.DeviceIdType.MESH


def dot(a, b):
    return jnp.dot(a, b, preferred_element_type=F32)


def iota(shape, dim):
    return lax.broadcasted_iota(jnp.int32, shape, dim)


def split3(v):
    a = v.astype(BF16).astype(F32)
    c = (v - a).astype(BF16).astype(F32)
    return a, c, v - a - c


def lanes(n):
    return -(-n // HD) * HD


class Links:
    def __init__(self, B, H):
        self.n = {"heads": H, "branch": B}
        self.me = {"heads": lax.axis_index("heads"), "branch": lax.axis_index("branch")}
        self.pending = []

    def to(self, axis, d):
        n, me = self.n[axis], self.me[axis]
        if axis == "heads" and n % 2 == 0:
            return lax.rem(me // 2 + d // 2, n // 2) * 2 + lax.rem(me + d % 2, 2)
        return lax.rem(me + d, n)

    def order(self, axis):
        n = self.n[axis]
        if axis == "heads":
            return list(range(n - 1, 0, -1))
        return sorted(range(1, n), key=lambda d: (-min(d, n - d), d))

    def greet(self):
        barrier = pltpu.get_barrier_semaphore()
        for axis in ("branch", "heads"):
            for d in self.order(axis):
                pl.semaphore_signal(barrier, 1, device_id={axis: self.to(axis, d)}, device_id_type=MESH)

    def greeted(self):
        pl.semaphore_wait(pltpu.get_barrier_semaphore(), self.n["heads"] + self.n["branch"] - 2)

    def push(self, src, dst, sems, k, axis, d):
        c = pltpu.make_async_remote_copy(
            src_ref=src, dst_ref=dst, send_sem=sems.at[0, k, d], recv_sem=sems.at[1, k, d],
            device_id={axis: self.to(axis, d)}, device_id_type=MESH,
        )
        c.start()
        self.pending.append(c)
        return c

    def drain(self):
        for c in self.pending:
            c.wait_send()
        self.pending = []


def attender(H, MR, h, q2, kvn, len_v, kv_v, keep):
    heads_all = q2.shape[0] // MR
    kw = kvn.shape[1] // 2
    kvh = kw // HD
    span = kv_v.shape[1]
    block_mask = iota((heads_all, kw), 0) // (heads_all // kvh) == iota((heads_all, kw), 1) // HD
    lane = iota((heads_all, HD), 1)
    pos = (h * span + iota((heads_all, span), 1)).astype(F32)
    scaling = HD ** (-0.5)
    is_first = h == 0

    def score(r):
        q = q2[pl.ds(r, heads_all, stride=MR), :]
        qb = jnp.where(block_mask, jnp.concatenate([q] * kvh, axis=1), 0.0)
        scores = lax.dot_general(qb.astype(BF16), kv_v[r, :, 0:kw], NT, preferred_element_type=F32)
        return qb, scores

    def finish(r, scored, mz):
        qb, scores = scored
        scores = scores * scaling
        valid = pos < jnp.concatenate([len_v[pl.ds(r, 1), :]] * (span // HD), axis=1)
        scores = jnp.where(valid, scores, NEG)
        s_new = jnp.sum(qb * kvn[pl.ds(r, 1), 0:kw], axis=1, keepdims=True) * scaling
        top = jnp.maximum(jnp.max(scores, axis=1, keepdims=True), jnp.where(is_first, s_new, NEG))
        probs = jnp.where(valid, jnp.exp(scores - top), 0.0).astype(BF16)
        p_new = jnp.where(is_first, jnp.exp(s_new - top), 0.0).astype(BF16).astype(F32)
        z = jnp.sum(probs.astype(F32), axis=1, keepdims=True) + p_new
        o = dot(probs, kv_v[r, :, kw:2 * kw])
        o = jnp.where(block_mask, o + p_new * kvn[pl.ds(r, 1), kw:2 * kw], 0.0)
        acc = o[:, 0:HD]
        for e in range(1, kvh):
            acc = acc + o[:, e * HD:(e + 1) * HD]
        gl = heads_all // H
        for i in range(H):
            keep[i, r] = acc[i * gl:(i + 1) * gl]
        return jnp.where(lane == r, top, jnp.where(lane == MR + r, z, mz))

    return score, finish


def mixer_kernel(
    cfg,
    res, arr_row, lens, gain, dt_bias, a_rate, skip, ssm_gain, w_dt,
    w_q, w_kv, w_x, w_z, w_wr, w_oa, w_os, kv, st,
    out_res, st_v,
    wq_v, wkv_v, wx_v, wz_v, wwr_v, wdt_v, woa_v, wos_v, kv_v,
    res_v, arr_v, gain_v, lens_v, bias_v, rate_v, skip_v, sg_v,
    xin, xg, sb, rb, own, qg, kvg, q2, kvn, wrn, len_v, ord_v, cols_v, wm,
    accs, accr, gss, gsr, at2, ge, ga, ssm_v, fs, fr,
    ssem, wsem, kvsem, stsem, asem, bsem, csem, dsem, esem, fsem,
):
    B, H, MR, NS = cfg
    R = B * MR
    links = Links(B, H)
    b, h = links.me["branch"], links.me["heads"]
    piece = res.shape[1]
    model = piece * H * B
    cq, ckv, cx, cz, cw = (w_q.shape[1], w_kv.shape[1], w_x.shape[1], w_z.shape[1], wwr_v.shape[1])
    o_sum = cq
    o_kv = o_sum + HD
    o_wr = o_kv + ckv
    o_dt = o_wr + cw
    hl = w_dt.shape[0]
    o_x = o_dt + lanes(3 * hl)
    o_z = o_x + cx
    total_cols = o_z + cz
    sp = cx // hl
    heads_all = cq * H // HD
    gl = cq // HD

    links.greet()
    small = [
        pltpu.make_async_copy(src, dst, ssem.at[i])
        for i, (src, dst) in enumerate((
            (res, res_v), (arr_row, arr_v), (gain, gain_v), (lens, lens_v), (dt_bias, bias_v), (a_rate, rate_v),
            (skip, skip_v), (ssm_gain, sg_v), (w_dt, wdt_v),
        ))
    ]
    for c in small[:3]:
        c.start()
    weights = [
        pltpu.make_async_copy(src, dst, wsem.at[i])
        for i, (src, dst) in enumerate(((w_q, wq_v), (w_kv, wkv_v), (w_wr, wwr_v), (w_x, wx_v), (w_z, wz_v), (w_os, wos_v), (w_oa, woa_v)))
    ]
    for c in weights[:2] + small[3:] + weights[2:5]:
        c.start()
    for c in small[:3]:
        c.wait()

    perm = (iota((R, R), 0) == arr_v[...]).astype(BF16)
    rows = dot(perm, res_v[...])
    ord_v[...] = rows
    wide = xin.shape[2]
    sums = split3(jnp.sum(rows * rows, axis=1, keepdims=True))
    tail = jnp.zeros((R, wide - piece), F32)
    for i, part in enumerate(sums):
        tail = jnp.where(iota(tail.shape, 1) == i, part, tail)
    xin[0, :, 0:piece] = (rows * gain_v[...].reshape(1, piece).astype(F32)).astype(BF16)
    xin[0, :, piece:wide] = tail.astype(BF16)

    links.greeted()
    got = [links.push(xin.at[0], xin.at[d], asem, 0, "heads", d) for d in links.order("heads")]
    state_in = [pltpu.make_async_copy(st.at[r], st_v.at[r], stsem.at[r]) for r in range(MR)]
    cache_in = [pltpu.make_async_copy(kv.at[r], kv_v.at[r], kvsem.at[r]) for r in range(MR)]
    for c in state_in + cache_in + weights[5:]:
        c.start()
    for c in small[3:]:
        c.wait()
    mine = (iota((MR, R), 1) == b * MR + iota((MR, R), 0)).astype(F32)
    len_v[...] = jnp.broadcast_to(jnp.sum(mine * lens_v[...].astype(F32), axis=1, keepdims=True), (MR, HD))
    for c in got:
        c.wait_recv()

    def slot(i):
        if H % 2 == 0:
            dx = lax.rem(h // 2 - i // 2 + H // 2, H // 2)
            dc = lax.rem(h - i % 2 + 2, 2)
            return dx * 2 + dc
        return lax.rem(h - i + H, H)

    sumsq = jnp.zeros((R, 1), F32)
    for i in range(H):
        part = xin[slot(i)]
        xg[:, i * piece:(i + 1) * piece] = part[:, 0:piece]
        t = part[:, piece:wide].astype(F32)
        sumsq = sumsq + jnp.sum(jnp.where(iota(t.shape, 1) < 3, t, 0.0), axis=1, keepdims=True)
    x = xg[...]

    def project(i, w_ref, lo, hi):
        weights[i].wait()
        val = dot(x, w_ref[...])
        own[:, lo:hi] = val
        for j in range(B):
            sb[j, :, lo:hi] = val[j * MR:(j + 1) * MR].astype(BF16)

    def scatter(k, lo, hi):
        return [
            links.push(sb.at[lax.rem(b + d, B), :, lo:hi], rb.at[d, :, lo:hi], bsem, k, "branch", d)
            for d in links.order("branch")
        ]

    def spread3(v, lo, hi):
        n = v.shape[1]
        val = jnp.zeros((R, hi - lo), F32)
        for i, part in enumerate(split3(v)):
            if n == 1:
                val = jnp.where(iota(val.shape, 1) == i, part, val)
            else:
                val = val + dot(part.astype(BF16), (iota((n, hi - lo), 1) == iota((n, hi - lo), 0) + i * n).astype(BF16))
        own[:, lo:hi] = val
        for j in range(B):
            sb[j, :, lo:hi] = val[j * MR:(j + 1) * MR].astype(BF16)

    spread3(sumsq, o_sum, o_kv)
    project(0, wq_v, 0, cq)
    got_q = scatter(0, 0, o_kv)
    project(1, wkv_v, o_kv, o_wr)
    got_kv = scatter(1, o_kv, o_wr)
    project(2, wwr_v, o_wr, o_dt)
    spread3(lax.dot_general(x, wdt_v[...], NT, preferred_element_type=F32), o_dt, o_x)
    got_wr = scatter(2, o_wr, o_x)
    project(3, wx_v, o_x, o_z)
    project(4, wz_v, o_z, total_cols)
    my_rows = pl.ds(pl.multiple_of(b * MR, MR), MR)
    for c in got_q:
        c.wait_recv()

    def gathered(lo, hi):
        val = own[my_rows, lo:hi]
        for d in range(1, B):
            val = val + rb[d, :, lo:hi].astype(F32)
        return val

    scale = lax.rsqrt(jnp.sum(gathered(o_sum, o_kv)[:, 0:3], axis=1, keepdims=True) / model + 1e-05)

    def reduced(lo, hi):
        return (gathered(lo, hi) * scale).astype(BF16)

    qg[h] = reduced(0, cq)
    got_a = [links.push(qg.at[h], qg.at[h], csem, 0, "heads", d) for d in links.order("heads")]
    for c in got_kv:
        c.wait_recv()
    kvg[h] = reduced(o_kv, o_wr)
    got_b = [links.push(kvg.at[h], kvg.at[h], csem, 1, "heads", d) for d in links.order("heads")]
    got_xz = scatter(3, o_x, total_cols)
    for c in got_wr:
        c.wait_recv()
    wrn[...] = reduced(o_wr, o_dt).astype(F32)
    write = wrn[:, 0:NS]
    read = wrn[:, NS:2 * NS]
    read_b = read.astype(BF16)
    row = iota((MR, cx), 0)
    for c in state_in:
        c.wait()

    def readout(r, y):
        part = lax.dot_general(read_b, st_v[r].astype(BF16), NT, preferred_element_type=F32)
        return jnp.where(row == r, part, y)

    y = lax.fori_loop(0, MR, readout, jnp.zeros((MR, cx), F32), unroll=2)
    dt_sum = gathered(o_dt, o_x)
    dt_raw = (dt_sum[:, 0:hl] + dt_sum[:, hl:2 * hl]) + dt_sum[:, 2 * hl:3 * hl]
    pre = dt_raw * scale + bias_v[...]
    step = jnp.maximum(pre, 0.0) + jnp.log1p(jnp.exp(-jnp.abs(pre)))
    decay = jnp.exp(-step * rate_v[...])
    spread = (iota((hl, cx), 1) // sp == iota((hl, cx), 0)).astype(F32)

    def widen(v):
        return jnp.dot(v, spread, preferred_element_type=F32, precision=lax.Precision.HIGHEST)

    decay_w = widen(decay)
    step_w = widen(step)
    skip_w = widen(jnp.broadcast_to(skip_v[...], (MR, hl)))
    for c in got_a:
        c.wait_recv()
    for g in range(heads_all):
        q2[g * MR:(g + 1) * MR, :] = qg[g // gl, :, (g % gl) * HD:(g % gl + 1) * HD].astype(F32)
    for c in got_b:
        c.wait_recv()
    for i in range(H):
        kvn[:, i * ckv:(i + 1) * ckv] = kvg[i].astype(F32)
    score, finish = attender(H, MR, h, q2, kvn, len_v, kv_v, accs)
    mz = jnp.zeros((heads_all, HD), F32)
    got = []
    for c in cache_in:
        c.wait()
    scored = score(0)
    first = MR - MR * 3 // 8
    for k in range(PARTS):
        lo, hi = ((0, first), (first, MR))[k]
        for r in range(lo, hi):
            later = score(r + 1) if r + 1 < MR else None
            mz = finish(r, scored, mz)
            scored = later
        end = hi
        if hi == MR:
            end = MR + 1
            for i in range(H):
                accs[i, MR] = mz[i * gl:(i + 1) * gl]
        for d in links.order("heads"):
            got.append(links.push(accs.at[links.to("heads", d), lo:end], accr.at[d, lo:end], dsem, k, "heads", d))
        if k == 0:
            for c in got_xz:
                c.wait_recv()
            ssm_x = reduced(o_x, o_z).astype(F32)
            ssm_z = reduced(o_z, total_cols).astype(F32)
            dtx = step_w * ssm_x
            y = decay_w * y + dtx * jnp.sum(write * read, axis=1, keepdims=True) + skip_w * ssm_x
            gated = y * (ssm_z * jax.nn.sigmoid(ssm_z))
            own_gate = jnp.broadcast_to(jnp.sum(gated * gated, axis=1, keepdims=True), (MR, HD))
            gss[...] = own_gate
            got_gate = [links.push(gss, gsr.at[d], dsem, PARTS, "heads", d) for d in links.order("heads")]
    for c in got_gate:
        c.wait_recv()
    gate = own_gate
    for d in range(1, H):
        gate = gate + gsr[d]
    ge[b] = (gated * lax.rsqrt(gate[:, 0:1] / (cx * H) + 1e-05) * sg_v[...]).astype(BF16)
    got_e = [links.push(ge.at[b], ge.at[b], esem, 0, "branch", d) for d in links.order("branch")]
    dtx_hi = dtx.astype(BF16).astype(F32)
    cols_v[...] = jnp.transpose(jnp.concatenate([dtx_hi, dtx - dtx_hi, decay_w], axis=0))
    turn = lax.rem(iota((2 * MR, NS), 0), MR)
    for r in range(MR):
        wm[:, r * NS:(r + 1) * NS] = jnp.where(turn == r, wrn[r:r + 1, 0:NS], 0.0).astype(BF16)
    def renew(i, carry):
        at = pl.multiple_of(i * sp, sp)
        lhs = cols_v[pl.ds(at, sp), 0:2 * MR].astype(BF16)
        keep = cols_v[pl.ds(at, 1), :]
        for r in range(MR):
            st_v[r, pl.ds(at, sp), :] = (
                keep[:, 2 * MR + r:2 * MR + r + 1] * st_v[r, pl.ds(at, sp), :] + dot(lhs, wm[:, r * NS:(r + 1) * NS])
            )
        return carry

    cut = hl // 2
    lax.fori_loop(0, cut, renew, 0, unroll=4 if cut % 4 == 0 else 1)
    for c in got:
        c.wait_recv()
    accr[0] = accs[h]
    mzr = [accr[i, MR] for i in range(H)]
    tops = [v[:, 0:MR] for v in mzr]
    best = functools.reduce(jnp.maximum, tops)
    shares = [jnp.exp(t - best) for t in tops]
    den = functools.reduce(jnp.add, [f * v[:, MR:2 * MR] for f, v in zip(shares, mzr)])
    for r in range(MR):
        num = functools.reduce(jnp.add, [f[:, r:r + 1] * accr[i, r] for i, f in enumerate(shares)])
        at2[pl.ds(r, gl, stride=MR), :] = num / den[:, r:r + 1]
    for g in range(gl):
        ga[b, :, g * HD:(g + 1) * HD] = at2[g * MR:(g + 1) * MR, :].astype(BF16)
    got_a = [links.push(ga.at[b], ga.at[b], esem, 1, "branch", d) for d in links.order("branch")]
    def stacked(ref):
        return jnp.concatenate([ref[i].astype(F32) for i in range(B)], axis=0)

    lax.fori_loop(cut, hl, renew, 0, unroll=4 if (hl - cut) % 4 == 0 else 1)
    for c in weights[5:]:
        c.wait()
    for c in got_e:
        c.wait_recv()
    ssm_v[...] = dot(stacked(ge).astype(BF16), wos_v[...])
    links.drain()
    for c in got_a:
        c.wait_recv()
    att = stacked(ga).astype(BF16)

    def send(d):
        return links.push(fs.at[links.to("heads", d)], fr.at[d], fsem, 0, "heads", d)

    got = []
    if H % 2 == 0 and 2 * piece % HD == 0:
        for dx in list(range(1, H // 2)) + [0]:
            chip = lax.rem(h // 2 + dx, H // 2)
            at = pl.ds(pl.multiple_of(chip * 2 * piece, HD), 2 * piece)
            part = dot(att, woa_v[:, at]) + ssm_v[:, at]
            for i in range(2):
                fs[chip * 2 + i] = part[:, i * piece:(i + 1) * piece].astype(fs.dtype)
            got += [send(d) for d in (2 * dx + 1, 2 * dx) if d > 0]
    else:
        part = dot(att, woa_v[...]) + ssm_v[...]
        for i in range(H):
            fs[i] = part[:, i * piece:(i + 1) * piece].astype(fs.dtype)
        got += [send(d) for d in links.order("heads")]
    total = ord_v[...] + fs[h].astype(F32)
    for c in got:
        c.wait_recv()
    for d in range(1, H):
        total = total + fr[d].astype(F32)
    out_res[...] = lax.dot_general(perm, total.astype(BF16), TN, preferred_element_type=F32).astype(BF16)
    links.drain()


def deliver_kernel(res, st, out_res, out_st, sem):
    copies = [pltpu.make_async_copy(res, out_res, sem.at[0])]
    for r in range(st.shape[0]):
        copies.append(pltpu.make_async_copy(st.at[r], out_st.at[r], sem.at[r + 1]))
    for c in copies:
        c.start()
    for c in copies:
        c.wait()


def body(
    B, H,
    residual, arrival, lengths, norm_gain, w_query, w_keyval, w_ssm_x, w_ssm_z, w_write_read, w_dt,
    dt_bias, a_rate, skip_gain, ssm_gain, w_out_att, w_out_ssm, kv_cache, ssm_state,
):
    R, piece = residual.shape
    MR = R // B
    width = piece * H
    cq, ckv, cx = w_query.shape[1], w_keyval.shape[1], w_ssm_x.shape[1]
    wr = w_write_read.shape[1]
    NS = wr // 2
    hl = w_dt.shape[1]
    cols = cq + wr + HD + ckv + 2 * cx + lanes(3 * hl)
    gl = cq // HD
    heads_all = gl * H
    wide = -(-(piece + 3) // 128) * 128
    st = ssm_state.reshape(MR, hl * ssm_state.shape[2], NS)
    vm = pl.BlockSpec(memory_space=pltpu.VMEM)
    hbm = pl.BlockSpec(memory_space=pltpu.HBM)
    dma = pltpu.SemaphoreType.DMA
    V = pltpu.VMEM
    scratch = [
        V(w_query.shape, BF16), V(w_keyval.shape, BF16), V(w_ssm_x.shape, BF16), V(w_ssm_z.shape, BF16),
        V(w_write_read.shape, BF16), V((hl, w_dt.shape[0]), BF16), V(w_out_att.shape, BF16), V(w_out_ssm.shape, BF16),
        V(kv_cache.shape, BF16),
        V((R, piece), BF16), V((1, R), jnp.int32), V(norm_gain.shape, BF16), V((1, R), jnp.int32),
        V((1, hl), F32), V((1, hl), F32), V((1, hl), F32), V((1, cx), F32),
        V((H, R, wide), BF16), V((R, width), BF16),
        V((B, MR, cols), BF16), V((B, MR, cols), BF16), V((R, cols), F32),
        V((H, MR, cq), BF16), V((H, MR, ckv), BF16),
        V((heads_all * MR, HD), F32), V((MR, ckv * H), F32), V((MR, wr), F32), V((MR, HD), F32), V((R, piece), F32),
        V((cx, 3 * MR), F32), V((2 * MR, MR * NS), BF16),
        V((H, MR + 1, gl, HD), F32), V((H, MR + 1, gl, HD), F32),
        V((MR, HD), F32), V((H, MR, HD), F32), V((gl * MR, HD), F32),
        V((B, MR, cx), BF16), V((B, MR, cq), BF16), V((R, piece * H), F32),
        V((H, R, piece), BF16), V((H, R, piece), BF16),
        dma((9,)), dma((7,)), dma((MR,)), dma((MR,)), dma((2, 1, H)), dma((2, 4, B)), dma((2, 2, H)),
        dma((2, PARTS + 1, H)), dma((2, 2, B)), dma((2, 1, H)),
    ]

    def near(*arrays):
        return [pltpu.with_memory_space_constraint(a, pltpu.VMEM) for a in arrays]

    def far(*arrays):
        return [pltpu.with_memory_space_constraint(a, pltpu.HBM) for a in arrays]

    out_res, new_state = pl.pallas_call(
        functools.partial(mixer_kernel, (B, H, MR, NS)),
        out_shape=(V((R, piece), BF16), V(st.shape, F32)),
        in_specs=[hbm] * 18,
        out_specs=(vm, vm),
        scratch_shapes=scratch,
        compiler_params=pltpu.CompilerParams(collective_id=0, has_side_effects=True, vmem_limit_bytes=50 * MIB),
        name="mixer",
    )(*far(
        residual, arrival.reshape(1, R), lengths.reshape(1, R), norm_gain,
        dt_bias.reshape(1, hl), a_rate.reshape(1, hl), skip_gain.reshape(1, hl), ssm_gain.reshape(1, cx), w_dt.T,
        w_query, w_keyval, w_ssm_x, w_ssm_z, w_write_read, w_out_att, w_out_ssm, kv_cache, st,
    ))
    out_res, new_state = pl.pallas_call(
        deliver_kernel,
        out_shape=(jax.ShapeDtypeStruct((R, piece), BF16), jax.ShapeDtypeStruct(st.shape, F32)),
        in_specs=[vm, vm],
        out_specs=(hbm, hbm),
        scratch_shapes=[dma((MR + 1,))],
        compiler_params=pltpu.CompilerParams(vmem_limit_bytes=16 * MIB),
        name="deliver",
    )(*near(out_res, new_state))
    return (out_res, new_state.reshape(ssm_state.shape))


def solution(mesh):
    return jax.shard_map(
        functools.partial(body, mesh.shape["branch"], mesh.shape["heads"]),
        mesh=mesh,
        in_specs=(
            P("parts", ("branch", "heads")),
            P("parts"),
            P("parts"),
            P(("branch", "heads")),
            P("branch", "heads"),
            P("branch", "heads"),
            P("branch", "heads"),
            P("branch", "heads"),
            P("branch", None),
            P("branch", "heads"),
            P("heads"),
            P("heads"),
            P("heads"),
            P("heads"),
            P("heads", "branch"),
            P("heads", "branch"),
            P(("parts", "branch"), "heads", None),
            P(("parts", "branch"), "heads", None, None),
        ),
        out_specs=(P("parts", ("branch", "heads")), P(("parts", "branch"), "heads", None, None)),
        check_vma=False,
    )
```

```python
import functools

import jax
import jax.numpy as jnp
from jax import lax
from jax.experimental import pallas as pl
from jax.experimental.pallas import tpu as pltpu
from jax.sharding import PartitionSpec as P

HD = 128
NEG = -1e30
PARTS = 2
F32 = jnp.float32
BF16 = jnp.bfloat16
MIB = 1024 * 1024
NT = (((1,), (1,)), ((), ()))
TN = (((0,), (0,)), ((), ()))
MESH = pl.DeviceIdType.MESH


def dot(a, b):
    return jnp.dot(a, b, preferred_element_type=F32)


def iota(shape, dim):
    return lax.broadcasted_iota(jnp.int32, shape, dim)


def split3(v):
    a = v.astype(BF16).astype(F32)
    c = (v - a).astype(BF16).astype(F32)
    return a, c, v - a - c


def lanes(n):
    return -(-n // HD) * HD


class Links:
    def __init__(self, B, H):
        self.n = {"heads": H, "branch": B}
        self.me = {"heads": lax.axis_index("heads"), "branch": lax.axis_index("branch")}
        self.pending = []

    def to(self, axis, d):
        n, me = self.n[axis], self.me[axis]
        if axis == "heads" and n % 2 == 0:
            return lax.rem(me // 2 + d // 2, n // 2) * 2 + lax.rem(me + d % 2, 2)
        return lax.rem(me + d, n)

    def order(self, axis):
        n = self.n[axis]
        if axis == "heads":
            return list(range(n - 1, 0, -1))
        return sorted(range(1, n), key=lambda d: (-min(d, n - d), d))

    def greet(self):
        barrier = pltpu.get_barrier_semaphore()
        for axis in ("branch", "heads"):
            for d in self.order(axis):
                pl.semaphore_signal(barrier, 1, device_id={axis: self.to(axis, d)}, device_id_type=MESH)

    def greeted(self):
        pl.semaphore_wait(pltpu.get_barrier_semaphore(), self.n["heads"] + self.n["branch"] - 2)

    def push(self, src, dst, sems, k, axis, d):
        c = pltpu.make_async_remote_copy(
            src_ref=src, dst_ref=dst, send_sem=sems.at[0, k, d], recv_sem=sems.at[1, k, d],
            device_id={axis: self.to(axis, d)}, device_id_type=MESH,
        )
        c.start()
        self.pending.append(c)
        return c

    def drain(self):
        for c in self.pending:
            c.wait_send()
        self.pending = []


def attender(H, MR, h, q2, kvn, len_v, kv_v, keep):
    heads_all = q2.shape[0] // MR
    kw = kvn.shape[1] // 2
    kvh = kw // HD
    span = kv_v.shape[1]
    block_mask = iota((heads_all, kw), 0) // (heads_all // kvh) == iota((heads_all, kw), 1) // HD
    lane = iota((heads_all, HD), 1)
    pos = (h * span + iota((heads_all, span), 1)).astype(F32)
    scaling = HD ** (-0.5)
    is_first = h == 0

    def score(r):
        q = q2[pl.ds(r, heads_all, stride=MR), :]
        qb = jnp.where(block_mask, jnp.concatenate([q] * kvh, axis=1), 0.0)
        scores = lax.dot_general(qb.astype(BF16), kv_v[r, :, 0:kw], NT, preferred_element_type=F32)
        return qb, scores

    def finish(r, scored, mz):
        qb, scores = scored
        scores = scores * scaling
        valid = pos < jnp.concatenate([len_v[pl.ds(r, 1), :]] * (span // HD), axis=1)
        scores = jnp.where(valid, scores, NEG)
        s_new = jnp.sum(qb * kvn[pl.ds(r, 1), 0:kw], axis=1, keepdims=True) * scaling
        top = jnp.maximum(jnp.max(scores, axis=1, keepdims=True), jnp.where(is_first, s_new, NEG))
        probs = jnp.where(valid, jnp.exp(scores - top), 0.0).astype(BF16)
        p_new = jnp.where(is_first, jnp.exp(s_new - top), 0.0).astype(BF16).astype(F32)
        z = jnp.sum(probs.astype(F32), axis=1, keepdims=True) + p_new
        o = dot(probs, kv_v[r, :, kw:2 * kw])
        o = jnp.where(block_mask, o + p_new * kvn[pl.ds(r, 1), kw:2 * kw], 0.0)
        acc = o[:, 0:HD]
        for e in range(1, kvh):
            acc = acc + o[:, e * HD:(e + 1) * HD]
        gl = heads_all // H
        for i in range(H):
            keep[i, r] = acc[i * gl:(i + 1) * gl]
        return jnp.where(lane == r, top, jnp.where(lane == MR + r, z, mz))

    return score, finish


def mixer_kernel(
    cfg,
    res, arr_row, lens, gain, dt_bias, a_rate, skip, ssm_gain, w_dt,
    w_q, w_kv, w_x, w_z, w_wr, w_oa, w_os, kv, st,
    out_res, st_v,
    wq_v, wkv_v, wx_v, wz_v, wwr_v, wdt_v, woa_v, wos_v, kv_v,
    res_v, arr_v, gain_v, lens_v, bias_v, rate_v, skip_v, sg_v,
    xin, xg, sb, rb, own, qg, kvg, q2, kvn, wrn, len_v, ord_v, cols_v, wm,
    accs, accr, gss, gsr, at2, ge, ga, ssm_v, fs, fr,
    ssem, wsem, kvsem, stsem, asem, bsem, csem, dsem, esem, fsem,
):
    B, H, MR, NS = cfg
    R = B * MR
    links = Links(B, H)
    b, h = links.me["branch"], links.me["heads"]
    piece = res.shape[1]
    model = piece * H * B
    cq, ckv, cx, cz, cw = (w_q.shape[1], w_kv.shape[1], w_x.shape[1], w_z.shape[1], wwr_v.shape[1])
    o_sum = cq
    o_kv = o_sum + HD
    o_wr = o_kv + ckv
    o_dt = o_wr + cw
    hl = w_dt.shape[0]
    o_x = o_dt + lanes(3 * hl)
    o_z = o_x + cx
    total_cols = o_z + cz
    sp = cx // hl
    heads_all = cq * H // HD
    gl = cq // HD

    small = [
        pltpu.make_async_copy(src, dst, ssem.at[i])
        for i, (src, dst) in enumerate((
            (res, res_v), (arr_row, arr_v), (gain, gain_v), (lens, lens_v), (dt_bias, bias_v), (a_rate, rate_v),
            (skip, skip_v), (ssm_gain, sg_v), (w_dt, wdt_v),
        ))
    ]
    for c in small[:3]:
        c.start()
    links.greet()
    weights = [
        pltpu.make_async_copy(src, dst, wsem.at[i])
        for i, (src, dst) in enumerate(((w_q, wq_v), (w_kv, wkv_v), (w_wr, wwr_v), (w_x, wx_v), (w_z, wz_v), (w_os, wos_v), (w_oa, woa_v)))
    ]
    for c in weights[:2] + small[3:] + weights[2:5]:
        c.start()
    for c in small[:3]:
        c.wait()

    perm = (iota((R, R), 0) == arr_v[...]).astype(BF16)
    rows = dot(perm, res_v[...])
    ord_v[...] = rows
    wide = xin.shape[2]
    sums = split3(jnp.sum(rows * rows, axis=1, keepdims=True))
    tail = jnp.zeros((R, wide - piece), F32)
    for i, part in enumerate(sums):
        tail = jnp.where(iota(tail.shape, 1) == i, part, tail)
    xin[0, :, 0:piece] = (rows * gain_v[...].reshape(1, piece).astype(F32)).astype(BF16)
    xin[0, :, piece:wide] = tail.astype(BF16)

    links.greeted()
    got = [links.push(xin.at[0], xin.at[d], asem, 0, "heads", d) for d in links.order("heads")]
    state_in = [pltpu.make_async_copy(st.at[r], st_v.at[r], stsem.at[r]) for r in range(MR)]
    cache_in = [pltpu.make_async_copy(kv.at[r], kv_v.at[r], kvsem.at[r]) for r in range(MR)]
    for c in state_in + cache_in:
        c.start()
    for c in small[3:]:
        c.wait()
    mine = (iota((MR, R), 1) == b * MR + iota((MR, R), 0)).astype(F32)
    len_v[...] = jnp.broadcast_to(jnp.sum(mine * lens_v[...].astype(F32), axis=1, keepdims=True), (MR, HD))
    for c in got:
        c.wait_recv()

    def slot(i):
        if H % 2 == 0:
            dx = lax.rem(h // 2 - i // 2 + H // 2, H // 2)
            dc = lax.rem(h - i % 2 + 2, 2)
            return dx * 2 + dc
        return lax.rem(h - i + H, H)

    sumsq = jnp.zeros((R, 1), F32)
    for i in range(H):
        part = xin[slot(i)]
        xg[:, i * piece:(i + 1) * piece] = part[:, 0:piece]
        t = part[:, piece:wide].astype(F32)
        sumsq = sumsq + jnp.sum(jnp.where(iota(t.shape, 1) < 3, t, 0.0), axis=1, keepdims=True)
    x = xg[...]

    def project(i, w_ref, lo, hi):
        weights[i].wait()
        val = dot(x, w_ref[...])
        own[:, lo:hi] = val
        for j in range(B):
            sb[j, :, lo:hi] = val[j * MR:(j + 1) * MR].astype(BF16)

    def scatter(k, lo, hi):
        return [
            links.push(sb.at[lax.rem(b + d, B), :, lo:hi], rb.at[d, :, lo:hi], bsem, k, "branch", d)
            for d in links.order("branch")
        ]

    def spread3(v, lo, hi):
        n = v.shape[1]
        val = jnp.zeros((R, hi - lo), F32)
        for i, part in enumerate(split3(v)):
            if n == 1:
                val = jnp.where(iota(val.shape, 1) == i, part, val)
            else:
                val = val + dot(part.astype(BF16), (iota((n, hi - lo), 1) == iota((n, hi - lo), 0) + i * n).astype(BF16))
        own[:, lo:hi] = val
        for j in range(B):
            sb[j, :, lo:hi] = val[j * MR:(j + 1) * MR].astype(BF16)

    spread3(sumsq, o_sum, o_kv)
    project(0, wq_v, 0, cq)
    got_q = scatter(0, 0, o_kv)
    project(1, wkv_v, o_kv, o_wr)
    got_kv = scatter(1, o_kv, o_wr)
    project(2, wwr_v, o_wr, o_dt)
    spread3(lax.dot_general(x, wdt_v[...], NT, preferred_element_type=F32), o_dt, o_x)
    got_wr = scatter(2, o_wr, o_x)
    project(3, wx_v, o_x, o_z)
    project(4, wz_v, o_z, total_cols)
    my_rows = pl.ds(pl.multiple_of(b * MR, MR), MR)
    for c in got_q:
        c.wait_recv()

    def gathered(lo, hi):
        val = own[my_rows, lo:hi]
        for d in range(1, B):
            val = val + rb[d, :, lo:hi].astype(F32)
        return val

    scale = lax.rsqrt(jnp.sum(gathered(o_sum, o_kv)[:, 0:3], axis=1, keepdims=True) / model + 1e-05)

    def reduced(lo, hi):
        return (gathered(lo, hi) * scale).astype(BF16)

    qg[h] = reduced(0, cq)
    got_a = [links.push(qg.at[h], qg.at[h], csem, 0, "heads", d) for d in links.order("heads")]
    for c in got_kv:
        c.wait_recv()
    kvg[h] = reduced(o_kv, o_wr)
    got_b = [links.push(kvg.at[h], kvg.at[h], csem, 1, "heads", d) for d in links.order("heads")]
    got_xz = scatter(3, o_x, total_cols)
    for c in got_wr:
        c.wait_recv()
    wrn[...] = reduced(o_wr, o_dt).astype(F32)
    write = wrn[:, 0:NS]
    read = wrn[:, NS:2 * NS]
    read_b = read.astype(BF16)
    row = iota((MR, cx), 0)
    for c in state_in:
        c.wait()

    def readout(r, y):
        part = lax.dot_general(read_b, st_v[r].astype(BF16), NT, preferred_element_type=F32)
        return jnp.where(row == r, part, y)

    y = lax.fori_loop(0, MR, readout, jnp.zeros((MR, cx), F32), unroll=2)
    dt_sum = gathered(o_dt, o_x)
    dt_raw = (dt_sum[:, 0:hl] + dt_sum[:, hl:2 * hl]) + dt_sum[:, 2 * hl:3 * hl]
    pre = dt_raw * scale + bias_v[...]
    step = jnp.maximum(pre, 0.0) + jnp.log1p(jnp.exp(-jnp.abs(pre)))
    decay = jnp.exp(-step * rate_v[...])
    spread = (iota((hl, cx), 1) // sp == iota((hl, cx), 0)).astype(F32)

    def widen(v):
        return jnp.dot(v, spread, preferred_element_type=F32, precision=lax.Precision.HIGHEST)

    decay_w = widen(decay)
    step_w = widen(step)
    skip_w = widen(jnp.broadcast_to(skip_v[...], (MR, hl)))
    for c in got_a:
        c.wait_recv()
    for g in range(heads_all):
        q2[g * MR:(g + 1) * MR, :] = qg[g // gl, :, (g % gl) * HD:(g % gl + 1) * HD].astype(F32)
    score, finish = attender(H, MR, h, q2, kvn, len_v, kv_v, accs)
    mz = jnp.zeros((heads_all, HD), F32)
    got = []
    cache_in[0].wait()
    scored = score(0)
    for c in cache_in[1:]:
        c.wait()
    for c in weights[5:]:
        c.start()
    for c in got_b:
        c.wait_recv()
    for i in range(H):
        kvn[:, i * ckv:(i + 1) * ckv] = kvg[i].astype(F32)
    first = MR - MR * 3 // 8
    for k in range(PARTS):
        lo, hi = ((0, first), (first, MR))[k]
        for r in range(lo, hi):
            if r + 1 < MR:
                later = score(r + 1)
            mz = finish(r, scored, mz)
            scored = later
        end = hi
        if hi == MR:
            end = MR + 1
            for i in range(H):
                accs[i, MR] = mz[i * gl:(i + 1) * gl]
        for d in links.order("heads"):
            got.append(links.push(accs.at[links.to("heads", d), lo:end], accr.at[d, lo:end], dsem, k, "heads", d))
        if k == 0:
            for c in got_xz:
                c.wait_recv()
            ssm_x = reduced(o_x, o_z).astype(F32)
            ssm_z = reduced(o_z, total_cols).astype(F32)
            dtx = step_w * ssm_x
            y = decay_w * y + dtx * jnp.sum(write * read, axis=1, keepdims=True) + skip_w * ssm_x
            gated = y * (ssm_z * jax.nn.sigmoid(ssm_z))
            own_gate = jnp.broadcast_to(jnp.sum(gated * gated, axis=1, keepdims=True), (MR, HD))
            gss[...] = own_gate
            got_gate = [links.push(gss, gsr.at[d], dsem, PARTS, "heads", d) for d in links.order("heads")]
    for c in got_gate:
        c.wait_recv()
    gate = own_gate
    for d in range(1, H):
        gate = gate + gsr[d]
    ge[b] = (gated * lax.rsqrt(gate[:, 0:1] / (cx * H) + 1e-05) * sg_v[...]).astype(BF16)
    got_e = [links.push(ge.at[b], ge.at[b], esem, 0, "branch", d) for d in links.order("branch")]
    dtx_hi = dtx.astype(BF16).astype(F32)
    cols_v[...] = jnp.transpose(jnp.concatenate([dtx_hi, dtx - dtx_hi, decay_w], axis=0))
    turn = lax.rem(iota((2 * MR, NS), 0), MR)
    for r in range(MR):
        wm[:, r * NS:(r + 1) * NS] = jnp.where(turn == r, wrn[r:r + 1, 0:NS], 0.0).astype(BF16)
    def renew(i, carry):
        at = pl.multiple_of(i * sp, sp)
        lhs = cols_v[pl.ds(at, sp), 0:2 * MR].astype(BF16)
        keep = cols_v[pl.ds(at, 1), :]
        for r in range(MR):
            st_v[r, pl.ds(at, sp), :] = (
                keep[:, 2 * MR + r:2 * MR + r + 1] * st_v[r, pl.ds(at, sp), :] + dot(lhs, wm[:, r * NS:(r + 1) * NS])
            )
        return carry

    cut = hl // 2
    lax.fori_loop(0, cut, renew, 0, unroll=4 if cut % 4 == 0 else 1)
    for c in got:
        c.wait_recv()
    accr[0] = accs[h]
    mzr = [accr[i, MR] for i in range(H)]
    tops = [v[:, 0:MR] for v in mzr]
    best = functools.reduce(jnp.maximum, tops)
    shares = [jnp.exp(t - best) for t in tops]
    den = functools.reduce(jnp.add, [f * v[:, MR:2 * MR] for f, v in zip(shares, mzr)])
    for r in range(MR):
        num = functools.reduce(jnp.add, [f[:, r:r + 1] * accr[i, r] for i, f in enumerate(shares)])
        at2[pl.ds(r, gl, stride=MR), :] = num / den[:, r:r + 1]
    for g in range(gl):
        ga[b, :, g * HD:(g + 1) * HD] = at2[g * MR:(g + 1) * MR, :].astype(BF16)
    got_a = [links.push(ga.at[b], ga.at[b], esem, 1, "branch", d) for d in links.order("branch")]
    def stacked(ref):
        return jnp.concatenate([ref[i].astype(F32) for i in range(B)], axis=0)

    lax.fori_loop(cut, hl, renew, 0, unroll=4 if (hl - cut) % 4 == 0 else 1)
    for c in weights[5:]:
        c.wait()
    for c in got_e:
        c.wait_recv()
    ssm_v[...] = dot(stacked(ge).astype(BF16), wos_v[...])
    links.drain()
    for c in got_a:
        c.wait_recv()
    att = stacked(ga).astype(BF16)

    def send(d):
        return links.push(fs.at[links.to("heads", d)], fr.at[d], fsem, 0, "heads", d)

    got = []
    if H % 2 == 0 and 2 * piece % HD == 0:
        for dx in list(range(1, H // 2)) + [0]:
            chip = lax.rem(h // 2 + dx, H // 2)
            at = pl.ds(pl.multiple_of(chip * 2 * piece, HD), 2 * piece)
            part = dot(att, woa_v[:, at]) + ssm_v[:, at]
            for i in range(2):
                fs[chip * 2 + i] = part[:, i * piece:(i + 1) * piece].astype(fs.dtype)
            got += [send(d) for d in (2 * dx + 1, 2 * dx) if d > 0]
    else:
        part = dot(att, woa_v[...]) + ssm_v[...]
        for i in range(H):
            fs[i] = part[:, i * piece:(i + 1) * piece].astype(fs.dtype)
        got += [send(d) for d in links.order("heads")]
    total = ord_v[...] + fs[h].astype(F32)
    for c in got:
        c.wait_recv()
    for d in range(1, H):
        total = total + fr[d].astype(F32)
    out_res[...] = lax.dot_general(perm, total.astype(BF16), TN, preferred_element_type=F32).astype(BF16)
    links.drain()


def deliver_kernel(res, st, out_res, out_st, sem):
    copies = [pltpu.make_async_copy(res, out_res, sem.at[0])]
    for r in range(st.shape[0]):
        copies.append(pltpu.make_async_copy(st.at[r], out_st.at[r], sem.at[r + 1]))
    for c in copies:
        c.start()
    for c in copies:
        c.wait()


def body(
    B, H,
    residual, arrival, lengths, norm_gain, w_query, w_keyval, w_ssm_x, w_ssm_z, w_write_read, w_dt,
    dt_bias, a_rate, skip_gain, ssm_gain, w_out_att, w_out_ssm, kv_cache, ssm_state,
):
    R, piece = residual.shape
    MR = R // B
    width = piece * H
    cq, ckv, cx = w_query.shape[1], w_keyval.shape[1], w_ssm_x.shape[1]
    wr = w_write_read.shape[1]
    NS = wr // 2
    hl = w_dt.shape[1]
    cols = cq + wr + HD + ckv + 2 * cx + lanes(3 * hl)
    gl = cq // HD
    heads_all = gl * H
    wide = -(-(piece + 3) // 128) * 128
    st = ssm_state.reshape(MR, hl * ssm_state.shape[2], NS)
    vm = pl.BlockSpec(memory_space=pltpu.VMEM)
    hbm = pl.BlockSpec(memory_space=pltpu.HBM)
    dma = pltpu.SemaphoreType.DMA
    V = pltpu.VMEM
    scratch = [
        V(w_query.shape, BF16), V(w_keyval.shape, BF16), V(w_ssm_x.shape, BF16), V(w_ssm_z.shape, BF16),
        V(w_write_read.shape, BF16), V((hl, w_dt.shape[0]), BF16), V(w_out_att.shape, BF16), V(w_out_ssm.shape, BF16),
        V(kv_cache.shape, BF16),
        V((R, piece), BF16), V((1, R), jnp.int32), V(norm_gain.shape, BF16), V((1, R), jnp.int32),
        V((1, hl), F32), V((1, hl), F32), V((1, hl), F32), V((1, cx), F32),
        V((H, R, wide), BF16), V((R, width), BF16),
        V((B, MR, cols), BF16), V((B, MR, cols), BF16), V((R, cols), F32),
        V((H, MR, cq), BF16), V((H, MR, ckv), BF16),
        V((heads_all * MR, HD), F32), V((MR, ckv * H), F32), V((MR, wr), F32), V((MR, HD), F32), V((R, piece), F32),
        V((cx, 3 * MR), F32), V((2 * MR, MR * NS), BF16),
        V((H, MR + 1, gl, HD), F32), V((H, MR + 1, gl, HD), F32),
        V((MR, HD), F32), V((H, MR, HD), F32), V((gl * MR, HD), F32),
        V((B, MR, cx), BF16), V((B, MR, cq), BF16), V((R, piece * H), F32),
        V((H, R, piece), BF16), V((H, R, piece), BF16),
        dma((9,)), dma((7,)), dma((MR,)), dma((MR,)), dma((2, 1, H)), dma((2, 4, B)), dma((2, 2, H)),
        dma((2, PARTS + 1, H)), dma((2, 2, B)), dma((2, 1, H)),
    ]

    def near(*arrays):
        return [pltpu.with_memory_space_constraint(a, pltpu.VMEM) for a in arrays]

    def far(*arrays):
        return [pltpu.with_memory_space_constraint(a, pltpu.HBM) for a in arrays]

    out_res, new_state = pl.pallas_call(
        functools.partial(mixer_kernel, (B, H, MR, NS)),
        out_shape=(V((R, piece), BF16), V(st.shape, F32)),
        in_specs=[hbm] * 18,
        out_specs=(vm, vm),
        scratch_shapes=scratch,
        compiler_params=pltpu.CompilerParams(collective_id=0, has_side_effects=True, vmem_limit_bytes=50 * MIB),
        name="mixer",
    )(*far(
        residual, arrival.reshape(1, R), lengths.reshape(1, R), norm_gain,
        dt_bias.reshape(1, hl), a_rate.reshape(1, hl), skip_gain.reshape(1, hl), ssm_gain.reshape(1, cx), w_dt.T,
        w_query, w_keyval, w_ssm_x, w_ssm_z, w_write_read, w_out_att, w_out_ssm, kv_cache, st,
    ))
    out_res, new_state = pl.pallas_call(
        deliver_kernel,
        out_shape=(jax.ShapeDtypeStruct((R, piece), BF16), jax.ShapeDtypeStruct(st.shape, F32)),
        in_specs=[vm, vm],
        out_specs=(hbm, hbm),
        scratch_shapes=[dma((MR + 1,))],
        compiler_params=pltpu.CompilerParams(vmem_limit_bytes=16 * MIB),
        name="deliver",
    )(*near(out_res, new_state))
    return (out_res, new_state.reshape(ssm_state.shape))


def solution(mesh):
    return jax.shard_map(
        functools.partial(body, mesh.shape["branch"], mesh.shape["heads"]),
        mesh=mesh,
        in_specs=(
            P("parts", ("branch", "heads")),
            P("parts"),
            P("parts"),
            P(("branch", "heads")),
            P("branch", "heads"),
            P("branch", "heads"),
            P("branch", "heads"),
            P("branch", "heads"),
            P("branch", None),
            P("branch", "heads"),
            P("heads"),
            P("heads"),
            P("heads"),
            P("heads"),
            P("heads", "branch"),
            P("heads", "branch"),
            P(("parts", "branch"), "heads", None),
            P(("parts", "branch"), "heads", None, None),
        ),
        out_specs=(P("parts", ("branch", "heads")), P(("parts", "branch"), "heads", None, None)),
        check_vma=False,
    )
```
